32 devices in a mesh: groups: 2 (over x), seq: 16 (over z, y, core).
Axes of the slice: x: 2, y: 2, z: 4, core: 2. Of those that a mesh axis runs over, the one named last changes fastest.
Arguments:
- queries: bfloat16 [256, 2560], P(('groups', 'seq')), parts along dimension 0, may hold values from -130 to 130
- cache_keys: bfloat16 [32768, 2560], P(('groups', 'seq')), parts along dimension 0, may hold values from -6 to 6
- cache_values: bfloat16 [32768, 2560], P(('groups', 'seq')), parts along dimension 0, may hold values from -6 to 6
- span_keys: bfloat16 [256, 2560], P(('groups', 'seq')), parts along dimension 0, may hold values from -8 to 8
- span_values: bfloat16 [256, 2560], P(('groups', 'seq')), parts along dimension 0, may hold values from -6 to 6
- cache_tokens: int32 [2], P('groups'), parts along dimension 0, may hold values from 8192 to 16384
- span_start: int32 [2], P('groups'), parts along dimension 0, may hold values from 1433 to 1559
Outputs:
- attended: bfloat16 [256, 2560], P(('groups', 'seq')), parts along dimension 0
The draws below stay inside these ranges and needn't reach their ends.
There are 2 independent parts, one for each index of `groups`. The reference program is written for one: setup_inputs(seed, part) draws one part's arguments, and reference() takes and returns one part's arrays. A program takes and returns all parts, laid end to end along the dimension named above; each array names one. Nothing has to cross between parts.
All inputs are finite; a program needn't handle non-finite values.
Results may differ from the reference program's by a relative error of at most 0.0026.
Values may be sent and summed in bfloat16 or wider, within the bound.
No kernel may reach another device: no remote copies, remote signals or barrier semaphores. Data moves between devices by JAX's collectives and lax.ppermute only.
A program may use at most 320 MiB of HBM per device.

```python
import math
import jax
import jax.numpy as jnp
from jax import lax

HEAD_DIM = 128
HEADS = 20
FRAME_TOK = 1560
CDEV = 1024
SPAN = 128
CACHE = 16384
N_SEQ = 16


def draw_queries(key, part):
    sample = 3.0 * jax.random.truncated_normal(jax.random.fold_in(key, 1), -6.0, 6.0, (SPAN, HEADS * HEAD_DIM), jnp.float32)
    return sample.astype(jnp.bfloat16)


def draw_cache_keys(key, part):
    sample = jax.random.truncated_normal(jax.random.fold_in(key, 2), -6.0, 6.0, (CACHE, HEADS * HEAD_DIM), jnp.float32)
    return sample.astype(jnp.bfloat16)


def block_levels(rng, dims, pieces, low, largest):
    def one(dim, shards_of):
        steps = jax.random.uniform(jax.random.fold_in(jax.random.fold_in(rng, 6), dim), (shards_of,), jnp.float32, low / len(pieces), largest / len(pieces))
        return jnp.repeat(jnp.exp(steps), dims[dim] // shards_of).reshape((-1,) + (1,) * (len(dims) - dim - 1))

    factor_of = one(*pieces[0])
    for cut in pieces[1:]:
        factor_of = factor_of * one(*cut)
    return factor_of


def bell_draw(stream_key, shape, spread, bound, cuts=(), kind=jnp.bfloat16):
    drawn = jax.random.normal(stream_key, shape, jnp.float32) * spread
    if len(cuts) > 0:
        drawn = block_levels(stream_key, shape, cuts, -0.22, 0.18) * drawn
    return jnp.clip(drawn, min=-bound, max=bound).astype(kind)


def setup_inputs(seed: int = 0, part: int = 0) -> dict:
    splits = jax.random.split(jax.random.key(seed), 8)
    part_splits = jax.random.split(jax.random.fold_in(splits[7], part), 8)
    queries = draw_queries(jax.random.fold_in(jax.random.fold_in(splits[7], part), 71), part)
    cache_keys = draw_cache_keys(jax.random.fold_in(jax.random.fold_in(splits[7], part), 71), part)
    cache_values = bell_draw(part_splits[2], (CACHE, HEADS * HEAD_DIM), 1.0, 6.0, ((0, 16),))
    span_keys = bell_draw(part_splits[3], (SPAN, HEADS * HEAD_DIM), 1.3, 8.0, ((0, 16),))
    span_values = bell_draw(part_splits[4], (SPAN, HEADS * HEAD_DIM), 1.0, 6.0, ((0, 16),))
    cache_tokens = jax.random.randint(part_splits[5], (1,), CACHE // 2, CACHE + 1).astype(jnp.int32)
    span_start = jax.random.randint(part_splits[6], (1,), FRAME_TOK - SPAN + 1, FRAME_TOK).astype(jnp.int32)
    return dict(queries=queries, cache_keys=cache_keys, cache_values=cache_values, span_keys=span_keys, span_values=span_values, cache_tokens=cache_tokens, span_start=span_start)


NEG_FILL = -1e+30

def reference(queries, cache_keys, cache_values, span_keys, span_values, cache_tokens, span_start):
    score_scale = 1.0 / math.sqrt(HEAD_DIM)
    query_heads = queries.astype(jnp.float32).reshape(SPAN, HEADS, HEAD_DIM)
    valid_end = cache_tokens[0]
    frame_of = (span_start[0] + jnp.arange(SPAN, dtype=jnp.int32)) // FRAME_TOK
    span_mask = frame_of[None, :] <= frame_of[:, None]
    own_keys = span_keys.astype(jnp.float32).reshape(SPAN, HEADS, HEAD_DIM)
    own_values = span_values.astype(jnp.float32).reshape(SPAN, HEADS, HEAD_DIM)
    span_scores = jnp.einsum('qhd,khd->hqk', query_heads, own_keys) * score_scale
    span_scores = jnp.where(span_mask[None], span_scores, NEG_FILL)
    key_blocks = cache_keys.reshape(N_SEQ, CDEV, HEADS, HEAD_DIM)
    value_blocks = cache_values.reshape(N_SEQ, CDEV, HEADS, HEAD_DIM)
    offsets = jnp.arange(N_SEQ, dtype=jnp.int32) * CDEV

    def block_scores(key_rows, offset):
        scores = jnp.einsum('qhd,khd->hqk', query_heads, key_rows.astype(jnp.float32)) * score_scale
        position = offset + jnp.arange(CDEV, dtype=jnp.int32)
        return jnp.where((position < valid_end)[None, None, :], scores, NEG_FILL)

    def max_step(running, block_item):
        key_rows, offset = block_item
        return (jnp.maximum(running, lax.optimization_barrier(jnp.max(block_scores(key_rows, offset), axis=2))), None)
    row_top, _ = lax.scan(max_step, lax.optimization_barrier(jnp.max(span_scores, axis=2)), (key_blocks, offsets))

    def weigh(scores, value_rows):
        weights = jnp.exp(scores - row_top[:, :, None])
        rounded = lax.optimization_barrier(weights.astype(jnp.bfloat16)).astype(jnp.float32)
        return (lax.optimization_barrier(jnp.sum(weights, axis=2)), jnp.einsum('hqk,khd->qhd', rounded, value_rows.astype(jnp.float32)))
    first_den, first_num = weigh(span_scores, own_values)

    def sum_step(running, block_item):
        key_rows, value_rows, offset = block_item
        part_den, part_num = weigh(block_scores(key_rows, offset), value_rows)
        return ((running[0] + part_den, running[1] + part_num), None)
    (denominator, numerator), _ = lax.scan(sum_step, (first_den, first_num), (key_blocks, value_blocks, offsets))
    attended = numerator / jnp.transpose(denominator)[:, :, None]
    return attended.reshape(SPAN, HEADS * HEAD_DIM).astype(jnp.bfloat16)
```

```python
import functools
import math

import jax
import jax.numpy as jnp
from jax import lax
from jax.experimental import pallas as pl
from jax.experimental.pallas import tpu as pltpu
from jax.sharding import PartitionSpec as P

HEAD_DIM = 128
HEADS = 20
FRAME_TOK = 1560
LANES = 128
PART = 32
NEG_FILL = -1e30
LOG_FLOOR = -30000.0
FIXED = 32768.0
HALF_RANGE = 32768
STEPS = 32512.0
PEAK_FLOOR = 1e-30
SCALE = math.log2(math.e) / math.sqrt(HEAD_DIM)
WIDTH = HEADS * HEAD_DIM
PER_STEP = 2


def pack(o):
    peak = jnp.max(jnp.abs(o), axis=1, keepdims=True)
    power = jnp.ceil(jnp.log2(jnp.maximum(peak, PEAK_FLOOR)))
    steps = jnp.round(o * (jnp.exp2(-power) * STEPS))
    return steps.astype(jnp.int32).astype(jnp.int16), power


def unpack(steps):
    return steps.astype(jnp.int32).astype(jnp.float32)


def pack_stats(log_sum, power):
    fixed = jnp.round(log_sum * FIXED).astype(jnp.int32)
    high = fixed // HALF_RANGE
    low = fixed - high * HALF_RANGE
    lane = lax.broadcasted_iota(jnp.int32, log_sum.shape, 1)
    packed = jnp.where(lane < PART, high, pltpu.roll(low, PART, 1))
    packed = jnp.where(lane < 2 * PART, packed, pltpu.roll(power.astype(jnp.int32), 2 * PART, 1))
    return packed.astype(jnp.int16)


def unpack_stats(packed):
    packed = packed.astype(jnp.int32)
    fixed = packed * HALF_RANGE + pltpu.roll(packed, LANES - PART, 1)
    power = pltpu.roll(packed, LANES - 2 * PART, 1)
    return fixed.astype(jnp.float32) * (1.0 / FIXED), power.astype(jnp.float32)


def attend_kernel(limit_ref, q_ref, k_ref, v_ref, sk_ref, sv_ref, qf_ref, kf_ref, keep_ref, keep_log_ref, send_ref, send_log_ref, logs, powers):
    step = pl.program_id(0)
    rows, keys = q_ref.shape[0], k_ref.shape[0]
    half = rows // 2
    used = limit_ref[0]
    slot = lax.broadcasted_iota(jnp.int32, (1, keys), 1)
    bias = jnp.where(slot < used, 0.0, NEG_FILL)
    span_bias = jnp.where(kf_ref[0:1, :] <= qf_ref[:, 0:1], 0.0, NEG_FILL)
    contract_last = (((1,), (1,)), ((), ()))
    @pl.when(step == 0)
    def _():
        logs[...] = jnp.zeros_like(logs)
        powers[...] = jnp.zeros_like(powers)

    for part in range(PER_STEP):
        cols = slice(part * HEAD_DIM, (part + 1) * HEAD_DIM)
        q = q_ref[:, cols]
        s = lax.dot_general(q, k_ref[:, cols], contract_last, preferred_element_type=jnp.float32) + bias
        s2 = lax.dot_general(q, sk_ref[:, cols], contract_last, preferred_element_type=jnp.float32) + span_bias
        top = jnp.maximum(jnp.max(s, axis=1, keepdims=True), jnp.max(s2, axis=1, keepdims=True))
        p = jnp.exp2((s - top) * SCALE)
        p2 = jnp.exp2((s2 - top) * SCALE)
        total = jnp.sum(p, axis=1, keepdims=True) + jnp.sum(p2, axis=1, keepdims=True)
        high = p.astype(jnp.bfloat16)
        low = (p - high.astype(jnp.float32)).astype(jnp.bfloat16)
        v = v_ref[:, cols]
        o = jnp.dot(high, v, preferred_element_type=jnp.float32) + jnp.dot(low, v, preferred_element_type=jnp.float32)
        high2 = p2.astype(jnp.bfloat16)
        low2 = (p2 - high2.astype(jnp.float32)).astype(jnp.bfloat16)
        sv = sv_ref[:, cols]
        o = o + jnp.dot(high2, sv, preferred_element_type=jnp.float32) + jnp.dot(low2, sv, preferred_element_type=jnp.float32)
        o = o * (1.0 / total)
        log_sum = jnp.maximum(top * SCALE + jnp.log2(total), LOG_FLOOR)
        keep_ref[:, cols] = o[:half]
        send_ref[:, cols], power = pack(o[half:])
        lane = lax.broadcasted_iota(jnp.int32, (rows, LANES), 1)
        logs[...] = jnp.where(lane == step * PER_STEP + part, log_sum, logs[...])
        powers[...] = jnp.where(lane[half:] == step * PER_STEP + part, power, powers[...])

    @pl.when(step == pl.num_programs(0) - 1)
    def _():
        keep_log_ref[...] = logs[:half, :]
        send_log_ref[...] = pack_stats(logs[half:, :], powers[...])


def attend(limit, q, k, v, sk, sv, query_frame, key_frame):
    rows, keys, own = q.shape[0], k.shape[0], sk.shape[0]
    half = rows // 2
    block = PER_STEP * HEAD_DIM
    column = lambda n: pl.BlockSpec((n, block), lambda i, *_: (0, i))
    whole = lambda shape: pl.BlockSpec(shape, lambda i, *_: (0, 0))
    return pl.pallas_call(
        attend_kernel,
        grid_spec=pltpu.PrefetchScalarGridSpec(
            num_scalar_prefetch=1,
            grid=(HEADS // PER_STEP,),
            in_specs=[column(rows), column(keys), column(keys), column(own), column(own), whole((rows, LANES)), whole((8, own))],
            out_specs=[column(half), whole((half, LANES)), column(half), whole((half, LANES))],
            scratch_shapes=[pltpu.VMEM((rows, LANES), jnp.float32), pltpu.VMEM((half, LANES), jnp.float32)],
        ),
        out_shape=[
            jax.ShapeDtypeStruct((half, WIDTH), jnp.float32),
            jax.ShapeDtypeStruct((half, LANES), jnp.float32),
            jax.ShapeDtypeStruct((half, WIDTH), jnp.int16),
            jax.ShapeDtypeStruct((half, LANES), jnp.int16),
        ],
        compiler_params=pltpu.CompilerParams(vmem_limit_bytes=24 << 20),
        name="attend",
    )(limit, q, k, v, sk, sv, query_frame, key_frame)


def merge_kernel(last, a_ref, a_log_ref, b_ref, b_log_ref, *outs):
    a_log = a_log_ref[...]
    b_log, b_power = unpack_stats(b_log_ref[...])
    top = jnp.maximum(a_log, b_log)
    a_weight, b_weight = jnp.exp2(a_log - top), jnp.exp2(b_log - top)
    total = a_weight + b_weight
    a_share, b_share = a_weight / total, b_weight / total * (jnp.exp2(b_power) * (1.0 / STEPS))
    rows = a_log.shape[0]
    half = rows if last else rows // 2
    lane = lax.broadcasted_iota(jnp.int32, (half, LANES), 1)
    powers = jnp.zeros((half, LANES), jnp.float32)
    for head in range(HEADS):
        cols = slice(head * HEAD_DIM, (head + 1) * HEAD_DIM)
        o = a_ref[:, cols] * a_share[:, head : head + 1] + unpack(b_ref[:, cols]) * b_share[:, head : head + 1]
        outs[0][:, cols] = o[:half].astype(outs[0].dtype)
        if not last:
            outs[2][:, cols], power = pack(o[half:])
            powers = jnp.where(lane == head, power, powers)
    if not last:
        log_sum = jnp.maximum(top + jnp.log2(total), LOG_FLOOR)
        outs[1][...] = log_sum[:half]
        outs[3][...] = pack_stats(log_sum[half:], powers)


def merge(a, a_log, b, b_log, last):
    rows = a.shape[0]
    half = rows // 2
    if last:
        shapes = [jax.ShapeDtypeStruct((rows, WIDTH), jnp.bfloat16)]
    else:
        shapes = [
            jax.ShapeDtypeStruct((half, WIDTH), jnp.float32),
            jax.ShapeDtypeStruct((half, LANES), jnp.float32),
            jax.ShapeDtypeStruct((half, WIDTH), jnp.int16),
            jax.ShapeDtypeStruct((half, LANES), jnp.int16),
        ]
    vmem = pl.BlockSpec(memory_space=pltpu.VMEM)
    return pl.pallas_call(
        functools.partial(merge_kernel, last),
        in_specs=[vmem] * 4,
        out_specs=[vmem] * len(shapes),
        out_shape=shapes,
        compiler_params=pltpu.CompilerParams(vmem_limit_bytes=16 << 20),
        name="merge",
    )(a, a_log, b, b_log)


def strides(devices):
    order = []
    stride = 2
    while stride < devices:
        order.append(stride)
        stride *= 2
    if len(order) >= 2:
        order = order[1:] + order[:1]
    return order + [1]


def local(devices, queries, cache_keys, cache_values, span_keys, span_values, cache_tokens, span_start):
    me = lax.axis_index("seq")
    cache_rows, own = cache_keys.shape[0], queries.shape[0]
    order = strides(devices)

    def swap(x, stride):
        return lax.ppermute(x, "seq", [(i, i ^ stride) for i in range(devices)])

    q, holder = queries, [0]
    for stride in order:
        q = jnp.concatenate([q, swap(q, stride)], axis=0)
        holder = holder + [h ^ stride for h in holder]
    position = (me ^ jnp.array(holder, jnp.int32))[:, None] * own + jnp.arange(own, dtype=jnp.int32)[None, :]
    query_frame = (span_start[0] + position.reshape(-1)) // FRAME_TOK
    query_frame = jnp.broadcast_to(query_frame[:, None], (devices * own, LANES))
    key_frame = (span_start[0] + me * own + jnp.arange(own, dtype=jnp.int32)) // FRAME_TOK
    key_frame = jnp.broadcast_to(key_frame[None, :], (8, own))
    limit = jnp.clip(cache_tokens - me * cache_rows, 0, cache_rows)
    keep, keep_log, send, send_log = attend(
        limit, q, cache_keys, cache_values, span_keys, span_values, query_frame, key_frame
    )
    for stride in order[:0:-1]:
        got, got_log = swap(send, stride), swap(send_log, stride)
        keep, keep_log, send, send_log = merge(keep, keep_log, got, got_log, False)
    got, got_log = swap(send, order[0]), swap(send_log, order[0])
    return merge(keep, keep_log, got, got_log, True)[0]


def solution(mesh):
    rows = P(("groups", "seq"), None)
    placed = (rows, rows, rows, rows, rows, P("groups"), P("groups"))
    return jax.shard_map(
        functools.partial(local, mesh.shape["seq"]), mesh=mesh, in_specs=placed, out_specs=rows, check_vma=False
    )
```

```python
import functools
import math

import jax
import jax.numpy as jnp
from jax import lax
from jax.experimental import pallas as pl
from jax.experimental.pallas import tpu as pltpu
from jax.sharding import PartitionSpec as P

HEAD_DIM = 128
HEADS = 20
FRAME_TOK = 1560
LANES = 128
PART = 32
NEG_FILL = -1e30
LOG_FLOOR = -30000.0
FIXED = 32768.0
HALF_RANGE = 32768
STEPS = 32512.0
PEAK_FLOOR = 1e-30
SCALE = math.log2(math.e) / math.sqrt(HEAD_DIM)
WIDTH = HEADS * HEAD_DIM


def pack(o):
    peak = jnp.max(jnp.abs(o), axis=1, keepdims=True)
    power = jnp.ceil(jnp.log2(jnp.maximum(peak, PEAK_FLOOR)))
    steps = jnp.round(o * (jnp.exp2(-power) * STEPS))
    return steps.astype(jnp.int32).astype(jnp.int16), power


def unpack(steps):
    return steps.astype(jnp.int32).astype(jnp.float32)


def pack_stats(log_sum, power):
    fixed = jnp.round(log_sum * FIXED).astype(jnp.int32)
    high = fixed // HALF_RANGE
    low = fixed - high * HALF_RANGE
    lane = lax.broadcasted_iota(jnp.int32, log_sum.shape, 1)
    packed = jnp.where(lane < PART, high, pltpu.roll(low, PART, 1))
    packed = jnp.where(lane < 2 * PART, packed, pltpu.roll(power.astype(jnp.int32), 2 * PART, 1))
    return packed.astype(jnp.int16)


def unpack_stats(packed):
    packed = packed.astype(jnp.int32)
    fixed = packed * HALF_RANGE + pltpu.roll(packed, LANES - PART, 1)
    power = pltpu.roll(packed, LANES - 2 * PART, 1)
    return fixed.astype(jnp.float32) * (1.0 / FIXED), power.astype(jnp.float32)


def attend_kernel(
    limit_ref, q_ref, k_hbm, v_hbm, sk_ref, sv_ref, qf_ref, kf_ref, keep_ref, keep_log_ref, send_ref, k_ref, v_ref, sems
):
    copies = []
    for head in range(HEADS):
        cols = pl.ds(head * HEAD_DIM, HEAD_DIM)
        pair = [
            pltpu.make_async_copy(k_hbm.at[:, cols], k_ref.at[:, cols], sems.at[head, 0]),
            pltpu.make_async_copy(v_hbm.at[:, cols], v_ref.at[:, cols], sems.at[head, 1]),
        ]
        for copy in pair:
            copy.start()
        copies.append(pair)
    rows, keys = q_ref.shape[0], k_ref.shape[0]
    half = rows // 2
    bias = jnp.where(lax.broadcasted_iota(jnp.int32, (1, keys), 1) < limit_ref[0], 0.0, NEG_FILL)
    span_bias = jnp.where(kf_ref[0:1, :] <= qf_ref[:, 0:1], 0.0, NEG_FILL)
    lane = lax.broadcasted_iota(jnp.int32, (rows, LANES), 1)
    logs = jnp.zeros((rows, LANES), jnp.float32)
    powers = jnp.zeros((rows - half, LANES), jnp.float32)
    contract_last = (((1,), (1,)), ((), ()))
    dot = functools.partial(jnp.dot, preferred_element_type=jnp.float32)
    for head in range(HEADS):
        cols = slice(head * HEAD_DIM, (head + 1) * HEAD_DIM)
        q = q_ref[:, cols]
        copies[head][0].wait()
        s = lax.dot_general(q, k_ref[:, cols], contract_last, preferred_element_type=jnp.float32) + bias
        s2 = lax.dot_general(q, sk_ref[:, cols], contract_last, preferred_element_type=jnp.float32) + span_bias
        top = jnp.maximum(jnp.max(s, axis=1, keepdims=True), jnp.max(s2, axis=1, keepdims=True))
        p = jnp.exp2((s - top) * SCALE)
        p2 = jnp.exp2((s2 - top) * SCALE)
        total = jnp.sum(p, axis=1, keepdims=True) + jnp.sum(p2, axis=1, keepdims=True)
        high, high2 = p.astype(jnp.bfloat16), p2.astype(jnp.bfloat16)
        low = (p - high.astype(jnp.float32)).astype(jnp.bfloat16)
        low2 = (p2 - high2.astype(jnp.float32)).astype(jnp.bfloat16)
        copies[head][1].wait()
        v, sv = v_ref[:, cols], sv_ref[:, cols]
        o = (dot(high, v) + dot(low, v) + dot(high2, sv) + dot(low2, sv)) * (1.0 / total)
        log_sum = jnp.maximum(top * SCALE + jnp.log2(total), LOG_FLOOR)
        keep_ref[:, cols] = o[:half]
        send_ref[:, cols], power = pack(o[half:])
        logs = jnp.where(lane == head, log_sum, logs)
        powers = jnp.where(lane[half:] == head, power, powers)
    keep_log_ref[...] = logs[:half]
    send_ref[:, WIDTH:] = pack_stats(logs[half:], powers)


def halves(rows):
    return [
        jax.ShapeDtypeStruct((rows, WIDTH), jnp.float32),
        jax.ShapeDtypeStruct((rows, LANES), jnp.float32),
        jax.ShapeDtypeStruct((rows, WIDTH + LANES), jnp.int16),
    ]


def attend(limit, q, k, v, sk, sv, query_frame, key_frame):
    vmem = pl.BlockSpec(memory_space=pltpu.VMEM)
    hbm = pl.BlockSpec(memory_space=pltpu.HBM)
    rows, keys = q.shape[0], k.shape[0]
    return pl.pallas_call(
        attend_kernel,
        in_specs=[pl.BlockSpec(memory_space=pltpu.SMEM), vmem, hbm, hbm] + [vmem] * 4,
        out_specs=[vmem] * 3,
        out_shape=halves(rows // 2),
        scratch_shapes=[
            pltpu.VMEM(k.shape, k.dtype),
            pltpu.VMEM(v.shape, v.dtype),
            pltpu.SemaphoreType.DMA((HEADS, 2)),
        ],
        compiler_params=pltpu.CompilerParams(vmem_limit_bytes=50 << 20),
        cost_estimate=pl.CostEstimate(
            flops=6 * rows * keys * WIDTH, bytes_accessed=4 * keys * WIDTH, transcendentals=rows * keys * HEADS
        ),
        name="attend",
    )(limit, q, k, v, sk, sv, query_frame, key_frame)


def merge_kernel(last, a_ref, a_log_ref, b_ref, *outs):
    a_log = a_log_ref[...]
    b_log, b_power = unpack_stats(b_ref[:, WIDTH:])
    top = jnp.maximum(a_log, b_log)
    a_weight, b_weight = jnp.exp2(a_log - top), jnp.exp2(b_log - top)
    total = a_weight + b_weight
    a_share, b_share = a_weight / total, b_weight / total * (jnp.exp2(b_power) * (1.0 / STEPS))
    rows = a_log.shape[0]
    half = rows if last else rows // 2
    lane = lax.broadcasted_iota(jnp.int32, (half, LANES), 1)
    powers = jnp.zeros((half, LANES), jnp.float32)
    for head in range(HEADS):
        cols = slice(head * HEAD_DIM, (head + 1) * HEAD_DIM)
        o = a_ref[:, cols] * a_share[:, head : head + 1] + unpack(b_ref[:, cols]) * b_share[:, head : head + 1]
        outs[0][:, cols] = o[:half].astype(outs[0].dtype)
        if not last:
            outs[2][:, cols], power = pack(o[half:])
            powers = jnp.where(lane == head, power, powers)
    if not last:
        log_sum = jnp.maximum(top + jnp.log2(total), LOG_FLOOR)
        outs[1][...] = log_sum[:half]
        outs[2][:, WIDTH:] = pack_stats(log_sum[half:], powers)


def merge(a, a_log, b, last):
    rows = a.shape[0]
    shapes = [jax.ShapeDtypeStruct((rows, WIDTH), jnp.bfloat16)] if last else halves(rows // 2)
    vmem = pl.BlockSpec(memory_space=pltpu.VMEM)
    return pl.pallas_call(
        functools.partial(merge_kernel, last),
        in_specs=[vmem] * 3,
        out_specs=[vmem] * len(shapes),
        out_shape=shapes,
        compiler_params=pltpu.CompilerParams(vmem_limit_bytes=16 << 20),
        name="merge",
    )(a, a_log, b)


def strides(devices):
    order = []
    stride = 2
    while stride < devices:
        order.append(stride)
        stride *= 2
    if len(order) >= 2:
        order = order[1:] + order[:1]
    return order + [1]


def local(devices, queries, cache_keys, cache_values, span_keys, span_values, cache_tokens, span_start):
    me = lax.axis_index("seq")
    cache_rows, own = cache_keys.shape[0], queries.shape[0]
    order = strides(devices)

    def swap(x, stride):
        return lax.ppermute(x, "seq", [(i, i ^ stride) for i in range(devices)])

    q, holder = queries, [0]
    for stride in order:
        q = lax.optimization_barrier(jnp.concatenate([q, swap(q, stride)], axis=0))
        holder = holder + [h ^ stride for h in holder]
    position = (me ^ jnp.array(holder, jnp.int32))[:, None] * own + jnp.arange(own, dtype=jnp.int32)[None, :]
    query_frame = (span_start[0] + position.reshape(-1)) // FRAME_TOK
    query_frame = jnp.broadcast_to(query_frame[:, None], (devices * own, LANES))
    key_frame = (span_start[0] + me * own + jnp.arange(own, dtype=jnp.int32)) // FRAME_TOK
    key_frame = jnp.broadcast_to(key_frame[None, :], (8, own))
    limit = jnp.clip(cache_tokens - me * cache_rows, 0, cache_rows)
    keep, keep_log, send = attend(
        limit, q, cache_keys, cache_values, span_keys, span_values, query_frame, key_frame
    )
    for stride in order[:0:-1]:
        keep, keep_log, send = merge(keep, keep_log, swap(send, stride), False)
    return merge(keep, keep_log, swap(send, order[0]), True)[0]


def solution(mesh):
    rows = P(("groups", "seq"), None)
    placed = (rows, rows, rows, rows, rows, P("groups"), P("groups"))
    return jax.shard_map(
        functools.partial(local, mesh.shape["seq"]), mesh=mesh, in_specs=placed, out_specs=rows, check_vma=False
    )
```

```python
import functools
import math

import jax
import jax.numpy as jnp
from jax import lax
from jax.experimental import pallas as pl
from jax.experimental.pallas import tpu as pltpu
from jax.sharding import PartitionSpec as P

HEAD_DIM = 128
HEADS = 20
FRAME_TOK = 1560
LANES = 128
PART = 32
NEG_FILL = -1e30
LOG_FLOOR = -30000.0
FIXED = 32768.0
HALF_RANGE = 32768
STEPS = 32512.0
PEAK_FLOOR = 1e-30
SCALE = math.log2(math.e) / math.sqrt(HEAD_DIM)
WIDTH = HEADS * HEAD_DIM
PAIR = 2 * HEAD_DIM
BLOCK = 128
CHUNK = 128
PAD = 16
LAST = (((1,), (1,)), ((), ()))
FIRST = (((0,), (0,)), ((), ()))


def power_of(peak):
    return jnp.ceil(jnp.log2(jnp.maximum(peak, PEAK_FLOOR)))


def pack(scaled):
    return jnp.round(scaled).astype(jnp.int32).astype(jnp.int16)


def unpack(steps):
    return steps.astype(jnp.int32).astype(jnp.float32)


def pack_stats(log_sum, power):
    fixed = jnp.round(log_sum * FIXED).astype(jnp.int32)
    high = fixed // HALF_RANGE
    low = fixed - high * HALF_RANGE
    lane = lax.broadcasted_iota(jnp.int32, log_sum.shape, 1)
    packed = jnp.where(lane < PART, high, pltpu.roll(low, PART, 1))
    packed = jnp.where(lane < 2 * PART, packed, pltpu.roll(power.astype(jnp.int32), 2 * PART, 1))
    return packed.astype(jnp.int16)


def unpack_stats(packed):
    packed = packed.astype(jnp.int32)
    fixed = packed * HALF_RANGE + pltpu.roll(packed, LANES - PART, 1)
    power = pltpu.roll(packed, LANES - 2 * PART, 1)
    return fixed.astype(jnp.float32) * (1.0 / FIXED), power.astype(jnp.float32)


def attend_kernel(
    limit_ref, q_ref, k_hbm, v_hbm, sk_ref, sv_ref, qf_ref, kf_ref, keep_ref, keep_stats_ref, send_ref,
    k_ref, v_ref, sems, bias_ref, s_even, s_odd, top_ref, logs_ref, powers_ref,
):
    rows, keys, own = q_ref.shape[0], k_ref.shape[1], sk_ref.shape[0]
    half = rows // 2
    pairs = HEADS // 2
    scores = (s_even, s_odd)

    def copy_of(pair, which):
        cols = pl.ds(pl.multiple_of(pair * PAIR, PAIR), PAIR)
        source, target = ((k_hbm, k_ref), (v_hbm, v_ref))[which]
        return pltpu.make_async_copy(source.at[:, cols], target.at[pair], sems.at[pair, which])

    for pair in range(pairs):
        copy_of(pair, 0).start()
        copy_of(pair, 1).start()
    logs_ref[...] = jnp.zeros_like(logs_ref)
    powers_ref[...] = jnp.zeros_like(powers_ref)
    slot = lax.broadcasted_iota(jnp.int32, bias_ref.shape, 0)
    bias_ref[...] = jnp.where(slot < limit_ref[0], 0.0, NEG_FILL)
    pad = jnp.zeros((PAD - own, PAIR), jnp.bfloat16)

    def block_at(block):
        again = not isinstance(block, int)
        first = pl.multiple_of(block * BLOCK, BLOCK) if again else block * BLOCK
        block_rows = pl.ds(first, BLOCK)
        span_bias = jnp.where(kf_ref[...] <= qf_ref[0:1, block_rows], 0.0, NEG_FILL)
        span_bias = jnp.concatenate([span_bias, span_bias], axis=1)

        def columns(pair):
            return pl.ds(pl.multiple_of(pair * PAIR, PAIR), PAIR)

        def score(pair, slot):
            cols = columns(pair)
            q = q_ref[block_rows, cols]
            zero = jnp.zeros((BLOCK, HEAD_DIM), q.dtype)
            q = jnp.concatenate(
                [jnp.concatenate([q[:, :HEAD_DIM], zero], 1), jnp.concatenate([zero, q[:, HEAD_DIM:]], 1)], 0
            )
            s2 = lax.dot_general(sk_ref[:, cols], q, LAST, preferred_element_type=jnp.float32) + span_bias
            scores[slot][keys:, :] = s2
            tops = s2
            for chunk in range(0, keys, CHUNK):
                part = pl.ds(chunk, CHUNK)
                s = lax.dot_general(k_ref[pair, part, :], q, LAST, preferred_element_type=jnp.float32)
                bias = bias_ref[part, :]
                s = s + jnp.concatenate([bias, bias], axis=1)
                scores[slot][part, :] = s
                tops = jnp.maximum(tops, jnp.max(s.reshape(CHUNK // 8, 8, PAIR), axis=0))
                yield
            top_ref[slot : slot + 1, :] = jnp.max(tops, axis=0, keepdims=True)

        def weigh(pair, slot, beside):
            cols = columns(pair)
            sv = jnp.concatenate([sv_ref[:, cols], pad], 0)
            top = top_ref[slot : slot + 1, :]
            outs = []
            for head in range(2):
                lanes = slice(head * HEAD_DIM, (head + 1) * HEAD_DIM)
                head_top = top[:, lanes]
                total = jnp.zeros((8, HEAD_DIM), jnp.float32)
                parts = []
                for chunk in list(range(0, keys, 2 * CHUNK)) + [keys]:
                    size = 2 * CHUNK if chunk < keys else own
                    if chunk < keys:
                        next(beside, None)
                    p = jnp.exp2((scores[slot][chunk : chunk + size, lanes] - head_top) * SCALE)
                    total = total + jnp.sum(p.reshape(size // 8, 8, HEAD_DIM), axis=0)
                    high = p.astype(jnp.bfloat16)
                    low = (p - high.astype(jnp.float32)).astype(jnp.bfloat16)
                    parts.append(jnp.concatenate([high, low], axis=1))
                both = lax.dot_general(
                    v_ref[pair, :, lanes], jnp.concatenate(parts[:-1], 0), FIRST, preferred_element_type=jnp.float32
                ) + lax.dot_general(
                    sv[:, lanes], jnp.concatenate([parts[-1], pad], 0), FIRST, preferred_element_type=jnp.float32
                )
                total = jnp.sum(total, axis=0, keepdims=True)
                o = (both[:, :HEAD_DIM] + both[:, HEAD_DIM:]) * (1.0 / total)
                power = power_of(jnp.max(jnp.abs(o), axis=0, keepdims=True))
                steps = jnp.exp2(-power) * STEPS
                if rows == BLOCK:
                    lane = lax.broadcasted_iota(jnp.int32, steps.shape, 1)
                    steps = jnp.where(lane < half, 1.0, steps)
                else:
                    steps = jnp.where(first < half, 1.0, steps)
                outs.append(jnp.transpose(o * steps))
                here = pl.ds(pair * 2 + head, 1)
                logs_ref[block, here, :] = jnp.maximum(head_top * SCALE + jnp.log2(total), LOG_FLOOR)
                powers_ref[block, here, :] = power
            for _ in beside:
                pass
            o = jnp.concatenate(outs, axis=1)
            if rows == BLOCK:
                keep_ref[:, cols] = o[:half]
                send_ref[:, cols] = pack(o[half:])
            else:
                @pl.when(first < half)
                def _():
                    keep_ref[block_rows, cols] = o

                @pl.when(first >= half)
                def _():
                    send_ref[pl.ds(pl.multiple_of(first - half, BLOCK), BLOCK), cols] = pack(o)

        def arrive(pair, which):
            if not again:
                copy_of(pair, which).wait()

        arrive(0, 0)
        for _ in score(0, 0):
            pass

        @pl.loop(0, pairs // 2 - 1)
        def _(twice):
            for slot in range(2):
                pair = twice * 2 + slot
                arrive(pair, 1)
                arrive(pair + 1, 0)
                weigh(pair, slot, score(pair + 1, 1 - slot))

        arrive(pairs - 2, 1)
        arrive(pairs - 1, 0)
        weigh(pairs - 2, 0, score(pairs - 1, 1))
        arrive(pairs - 1, 1)
        weigh(pairs - 1, 1, iter(()))

    block_at(0)
    if rows > BLOCK:
        pl.loop(1, rows // BLOCK)(block_at)
    for block in range(rows // BLOCK):
        logs, powers = jnp.transpose(logs_ref[block]), jnp.transpose(powers_ref[block])
        here = slice(block * BLOCK, min((block + 1) * BLOCK, half))
        kept = max(here.stop - here.start, 0)
        if kept:
            keep_stats_ref[here, :] = join_stats(logs[:kept], powers[:kept])
        if kept < BLOCK:
            there = slice(block * BLOCK + kept - half, (block + 1) * BLOCK - half)
            send_ref[there, WIDTH:] = pack_stats(logs[kept:], powers[kept:])


def join_stats(log_sum, power):
    lane = lax.broadcasted_iota(jnp.int32, log_sum.shape, 1)
    return jnp.where(lane < PART, log_sum, pltpu.roll(power, PART, 1))


def halves(rows):
    return [
        jax.ShapeDtypeStruct((rows, WIDTH), jnp.float32),
        jax.ShapeDtypeStruct((rows, LANES), jnp.float32),
        jax.ShapeDtypeStruct((rows, WIDTH + LANES), jnp.int16),
    ]


def attend(limit, q, k, v, sk, sv, query_frame, key_frame):
    vmem = pl.BlockSpec(memory_space=pltpu.VMEM)
    hbm = pl.BlockSpec(memory_space=pltpu.HBM)
    rows, keys, own = q.shape[0], k.shape[0], sk.shape[0]
    pairs = HEADS // 2
    return pl.pallas_call(
        attend_kernel,
        in_specs=[pl.BlockSpec(memory_space=pltpu.SMEM), vmem, hbm, hbm] + [vmem] * 4,
        out_specs=[vmem] * 3,
        out_shape=halves(rows // 2),
        scratch_shapes=[
            pltpu.VMEM((pairs, keys, PAIR), k.dtype),
            pltpu.VMEM((pairs, keys, PAIR), v.dtype),
            pltpu.SemaphoreType.DMA((pairs, 2)),
            pltpu.VMEM((keys, LANES), jnp.float32),
            pltpu.VMEM((keys + own, PAIR), jnp.float32),
            pltpu.VMEM((keys + own, PAIR), jnp.float32),
            pltpu.VMEM((8, PAIR), jnp.float32),
            pltpu.VMEM((rows // BLOCK, LANES, BLOCK), jnp.float32),
            pltpu.VMEM((rows // BLOCK, LANES, BLOCK), jnp.float32),
        ],
        compiler_params=pltpu.CompilerParams(vmem_limit_bytes=50 << 20),
        cost_estimate=pl.CostEstimate(
            flops=6 * rows * keys * WIDTH, bytes_accessed=4 * keys * WIDTH, transcendentals=rows * keys * HEADS
        ),
        name="attend",
    )(limit, q, k, v, sk, sv, query_frame, key_frame)


def merge_kernel(last, a_ref, a_stats_ref, b_ref, *outs):
    a_log = a_stats_ref[...]
    a_power = pltpu.roll(a_log, LANES - PART, 1)
    b_log, b_power = unpack_stats(b_ref[:, WIDTH:])
    rows = a_log.shape[0]
    half = rows if last else rows // 2
    top = jnp.maximum(a_log, b_log)
    a_weight, b_weight = jnp.exp2(a_log - top), jnp.exp2(b_log - top)
    total = a_weight + b_weight
    a_share, b_share = a_weight / total, b_weight / total * (jnp.exp2(b_power) * (1.0 / STEPS))
    if not last:
        power = jnp.maximum(a_power, b_power)
        row = lax.broadcasted_iota(jnp.int32, power.shape, 0)
        steps = jnp.where(row < half, 1.0, jnp.exp2(-power) * STEPS)
        a_share, b_share = a_share * steps, b_share * steps
    for head in range(HEADS):
        cols = slice(head * HEAD_DIM, (head + 1) * HEAD_DIM)
        o = a_ref[:, cols] * a_share[:, head : head + 1] + unpack(b_ref[:, cols]) * b_share[:, head : head + 1]
        outs[0][:, cols] = o[:half].astype(outs[0].dtype)
        if not last:
            outs[2][:, cols] = pack(o[half:])
    if not last:
        log_sum = jnp.maximum(top + jnp.log2(total), LOG_FLOOR)
        outs[1][...] = join_stats(log_sum[:half], power[:half])
        outs[2][:, WIDTH:] = pack_stats(log_sum[half:], power[half:])


def merge(a, a_stats, b, last):
    rows = a.shape[0]
    shapes = [jax.ShapeDtypeStruct((rows, WIDTH), jnp.bfloat16)] if last else halves(rows // 2)
    vmem = pl.BlockSpec(memory_space=pltpu.VMEM)
    return pl.pallas_call(
        functools.partial(merge_kernel, last),
        in_specs=[vmem] * 3,
        out_specs=[vmem] * len(shapes),
        out_shape=shapes,
        compiler_params=pltpu.CompilerParams(vmem_limit_bytes=16 << 20),
        name="merge",
    )(a, a_stats, b)


def strides(devices):
    order = []
    stride = 2
    while stride < devices:
        order.append(stride)
        stride *= 2
    if len(order) >= 2:
        order = order[1:] + order[:1]
    return order + [1]


def local(devices, queries, cache_keys, cache_values, span_keys, span_values, cache_tokens, span_start):
    me = lax.axis_index("seq")
    cache_rows, own = cache_keys.shape[0], queries.shape[0]
    order = strides(devices)

    def swap(x, stride):
        return lax.ppermute(x, "seq", [(i, i ^ stride) for i in range(devices)])

    q, holder = queries, [0]
    for stride in order:
        q = lax.optimization_barrier(jnp.concatenate([q, swap(q, stride)], axis=0))
        holder = holder + [h ^ stride for h in holder]
    position = (me ^ jnp.array(holder, jnp.int32))[:, None] * own + jnp.arange(own, dtype=jnp.int32)[None, :]
    query_frame = (span_start[0] + position.reshape(-1)) // FRAME_TOK
    query_frame = jnp.broadcast_to(query_frame[None, :], (8, devices * own))
    key_frame = (span_start[0] + me * own + jnp.arange(own, dtype=jnp.int32)) // FRAME_TOK
    key_frame = jnp.broadcast_to(key_frame[:, None], (own, LANES))
    limit = jnp.clip(cache_tokens - me * cache_rows, 0, cache_rows)
    keep, keep_stats, send = attend(
        limit, q, cache_keys, cache_values, span_keys, span_values, query_frame, key_frame
    )
    for stride in order[:0:-1]:
        keep, keep_stats, send = merge(keep, keep_stats, swap(send, stride), False)
    return merge(keep, keep_stats, swap(send, order[0]), True)[0]


def solution(mesh):
    rows = P(("groups", "seq"), None)
    placed = (rows, rows, rows, rows, rows, P("groups"), P("groups"))
    return jax.shard_map(
        functools.partial(local, mesh.shape["seq"]), mesh=mesh, in_specs=placed, out_specs=rows, check_vma=False
    )
```

```python
import functools
import math

import jax
import jax.numpy as jnp
from jax import lax
from jax.experimental import pallas as pl
from jax.experimental.pallas import tpu as pltpu
from jax.sharding import PartitionSpec as P

HEAD_DIM = 128
HEADS = 20
FRAME_TOK = 1560
LANES = 128
PART = 32
NEG_FILL = -1e30
LOG_FLOOR = -30000.0
FIXED = 32768.0
HALF_RANGE = 32768
STEPS = 32512.0
PEAK_FLOOR = 1e-30
SCALE = math.log2(math.e) / math.sqrt(HEAD_DIM)
WIDTH = HEADS * HEAD_DIM
GROUPS = 2
PART_HEADS = HEADS // GROUPS
PART_WIDTH = PART_HEADS * HEAD_DIM
PAIR = 2 * HEAD_DIM
BLOCK = 128
KEY_STEP = 512
WEIGHT_STEP = 256
STAGES = (1, 4, 7)
PAD = 16
LAST = (((1,), (1,)), ((), ()))
FIRST = (((0,), (0,)), ((), ()))


def power_of(peak):
    return jnp.ceil(jnp.log2(jnp.maximum(peak, PEAK_FLOOR)))


def pack(scaled):
    return jnp.round(scaled).astype(jnp.int32).astype(jnp.int16)


def unpack(steps):
    return steps.astype(jnp.int32).astype(jnp.float32)


def pack_stats(log_sum, power):
    fixed = jnp.round(log_sum * FIXED).astype(jnp.int32)
    high = fixed // HALF_RANGE
    low = fixed - high * HALF_RANGE
    lane = lax.broadcasted_iota(jnp.int32, log_sum.shape, 1)
    packed = jnp.where(lane < PART, high, pltpu.roll(low, PART, 1))
    packed = jnp.where(lane < 2 * PART, packed, pltpu.roll(power.astype(jnp.int32), 2 * PART, 1))
    return packed.astype(jnp.int16)


def unpack_stats(packed):
    packed = packed.astype(jnp.int32)
    fixed = packed * HALF_RANGE + pltpu.roll(packed, LANES - PART, 1)
    power = pltpu.roll(packed, LANES - 2 * PART, 1)
    return fixed.astype(jnp.float32) * (1.0 / FIXED), power.astype(jnp.float32)


def attend_kernel(
    limit_ref, q_ref, k_hbm, v_hbm, sk_ref, sv_ref, qf_ref, kf_ref, *refs
):
    results, refs = refs[: 3 * GROUPS], refs[3 * GROUPS :]
    k_ref, v_ref, sems, bias_ref, s_even, s_odd, top_ref, logs_ref, powers_ref = refs
    rows, keys, own = q_ref.shape[0], k_ref.shape[1], sk_ref.shape[0]
    half = rows // 2
    pairs = HEADS // 2
    scores = (s_even, s_odd)

    def copy_of(pair, which):
        cols = pl.ds(pair * PAIR, PAIR)
        source, target = ((k_hbm, k_ref), (v_hbm, v_ref))[which]
        return pltpu.make_async_copy(source.at[:, cols], target.at[pair], sems.at[pair, which])

    for pair in range(pairs):
        copy_of(pair, 0).start()
        copy_of(pair, 1).start()
    logs_ref[...] = jnp.zeros_like(logs_ref)
    powers_ref[...] = jnp.zeros_like(powers_ref)
    slot = lax.broadcasted_iota(jnp.int32, bias_ref.shape, 0)
    bias_ref[...] = jnp.where(slot < limit_ref[0], 0.0, NEG_FILL)
    pad = jnp.zeros((PAD - own, PAIR), jnp.bfloat16)

    def block_at(block):
        first = block * BLOCK if rows == BLOCK else pl.multiple_of(block * BLOCK, BLOCK)
        block_rows = pl.ds(first, BLOCK)
        span_bias = jnp.where(kf_ref[...] <= qf_ref[0:1, block_rows], 0.0, NEG_FILL)
        span_bias = jnp.concatenate([span_bias, span_bias], axis=1)

        def columns(pair):
            return slice(pair * PAIR, (pair + 1) * PAIR)

        def score(pair, slot):
            cols = columns(pair)
            q = q_ref[block_rows, cols]
            zero = jnp.zeros((BLOCK, HEAD_DIM), q.dtype)
            q = jnp.concatenate(
                [jnp.concatenate([q[:, :HEAD_DIM], zero], 1), jnp.concatenate([zero, q[:, HEAD_DIM:]], 1)], 0
            )
            s2 = lax.dot_general(sk_ref[:, cols], q, LAST, preferred_element_type=jnp.float32) + span_bias
            scores[slot][keys:, :] = s2
            tops = s2
            for chunk in range(0, keys, KEY_STEP):
                part = pl.ds(chunk, KEY_STEP)
                s = lax.dot_general(k_ref[pair, part, :], q, LAST, preferred_element_type=jnp.float32)
                bias = bias_ref[part, :]
                s = s + jnp.concatenate([bias, bias], axis=1)
                scores[slot][part, :] = s
                tops = jnp.maximum(tops, jnp.max(s.reshape(KEY_STEP // 8, 8, PAIR), axis=0))
                yield
            top_ref[slot : slot + 1, :] = jnp.max(tops, axis=0, keepdims=True)

        def weigh(pair, head, slot, beside, finish):
            cols = columns(pair)
            lanes = slice(head * HEAD_DIM, (head + 1) * HEAD_DIM)
            top = top_ref[slot : slot + 1, lanes]
            total = jnp.zeros((8, HEAD_DIM), jnp.float32)
            parts = []
            for chunk in list(range(0, keys, WEIGHT_STEP)) + [keys]:
                size = WEIGHT_STEP if chunk < keys else own
                if chunk < keys:
                    next(beside, None)
                    next(finish, None)
                p = jnp.exp2((scores[slot][chunk : chunk + size, lanes] - top) * SCALE)
                total = total + jnp.sum(p.reshape(size // 8, 8, HEAD_DIM), axis=0)
                high = p.astype(jnp.bfloat16)
                low = (p - high.astype(jnp.float32)).astype(jnp.bfloat16)
                parts.append(jnp.concatenate([high, low], axis=1))
            for _ in finish:
                pass
            sv = jnp.concatenate([sv_ref[:, cols], pad], 0)
            both = lax.dot_general(
                v_ref[pair, :, lanes], jnp.concatenate(parts[:-1], 0), FIRST, preferred_element_type=jnp.float32
            ) + lax.dot_general(
                sv[:, lanes], jnp.concatenate([parts[-1], pad], 0), FIRST, preferred_element_type=jnp.float32
            )
            return both, jnp.sum(total, axis=0, keepdims=True), top

        def place(pair, head, both, total, top):
            group, within = divmod(pair * 2 + head, PART_HEADS)
            cols = slice(within * HEAD_DIM, (within + 1) * HEAD_DIM)
            keep_ref, _, send_ref = results[3 * group : 3 * group + 3]
            o = (both[:, :HEAD_DIM] + both[:, HEAD_DIM:]) * (1.0 / total)
            power = power_of(jnp.max(jnp.abs(o), axis=0, keepdims=True))
            steps = jnp.exp2(-power) * STEPS
            lane = lax.broadcasted_iota(jnp.int32, steps.shape, 1)
            steps = jnp.where(first + lane < half, 1.0, steps)
            number = group * (LANES // GROUPS) + within
            logs_ref[block, number : number + 1, :] = jnp.maximum(top * SCALE + jnp.log2(total), LOG_FLOOR)
            powers_ref[block, number : number + 1, :] = power
            yield
            o = jnp.transpose(o * steps)
            yield
            if rows == BLOCK:
                keep_ref[:, cols] = o[:half]
                send_ref[:, cols] = pack(o[half:])
            else:
                @pl.when(first < half)
                def _():
                    keep_ref[block_rows, cols] = o

                @pl.when(first >= half)
                def _():
                    send_ref[pl.ds(pl.multiple_of(first - half, BLOCK), BLOCK), cols] = pack(o)

        def arrive(key_pairs, value_pairs):
            def wait():
                for pair in key_pairs:
                    if pair < pairs:
                        copy_of(pair, 0).wait()
                for pair in value_pairs:
                    copy_of(pair, 1).wait()

            wait() if rows == BLOCK else pl.when(block == 0)(wait)

        finish = iter(())
        arrive([0, 1], [0])
        for _ in score(0, 0):
            pass
        for pair in range(pairs):
            if pair in STAGES:
                until = min([p for p in STAGES if p > pair] + [pairs])
                arrive(range(pair + 1, until + 1), range(pair, until))
            beside = score(pair + 1, (pair + 1) % 2) if pair + 1 < pairs else iter(())
            for head in range(2):
                done = weigh(pair, head, pair % 2, beside, finish)
                finish = place(pair, head, *done)
            for _ in beside:
                pass
        for _ in finish:
            pass

    if rows == BLOCK:
        block_at(0)
    else:
        pl.loop(0, rows // BLOCK)(block_at)
    for block in range(rows // BLOCK):
        logs, powers = jnp.transpose(logs_ref[block]), jnp.transpose(powers_ref[block])
        here = slice(block * BLOCK, min((block + 1) * BLOCK, half))
        kept = max(here.stop - here.start, 0)
        for group in range(GROUPS):
            _, keep_stats_ref, send_ref = results[3 * group : 3 * group + 3]
            if group:
                logs, powers = (pltpu.roll(x, LANES - LANES // GROUPS, 1) for x in (logs, powers))
            if kept:
                keep_stats_ref[here, :] = join_stats(logs[:kept], powers[:kept])
            if kept < BLOCK:
                there = slice(block * BLOCK + kept - half, (block + 1) * BLOCK - half)
                send_ref[there, PART_WIDTH:] = pack_stats(logs[kept:], powers[kept:])


def join_stats(log_sum, power):
    lane = lax.broadcasted_iota(jnp.int32, log_sum.shape, 1)
    return jnp.where(lane < PART, log_sum, pltpu.roll(power, PART, 1))


def halves(rows):
    return [
        jax.ShapeDtypeStruct((rows, PART_WIDTH), jnp.float32),
        jax.ShapeDtypeStruct((rows, LANES), jnp.float32),
        jax.ShapeDtypeStruct((rows, PART_WIDTH + LANES), jnp.int16),
    ]


def attend(limit, q, k, v, sk, sv, query_frame, key_frame):
    vmem = pl.BlockSpec(memory_space=pltpu.VMEM)
    hbm = pl.BlockSpec(memory_space=pltpu.HBM)
    rows, keys, own = q.shape[0], k.shape[0], sk.shape[0]
    pairs = HEADS // 2
    return pl.pallas_call(
        attend_kernel,
        in_specs=[pl.BlockSpec(memory_space=pltpu.SMEM), vmem, hbm, hbm] + [vmem] * 4,
        out_specs=[vmem] * (3 * GROUPS),
        out_shape=halves(rows // 2) * GROUPS,
        scratch_shapes=[
            pltpu.VMEM((pairs, keys, PAIR), k.dtype),
            pltpu.VMEM((pairs, keys, PAIR), v.dtype),
            pltpu.SemaphoreType.DMA((pairs, 2)),
            pltpu.VMEM((keys, LANES), jnp.float32),
            pltpu.VMEM((keys + own, PAIR), jnp.float32),
            pltpu.VMEM((keys + own, PAIR), jnp.float32),
            pltpu.VMEM((8, PAIR), jnp.float32),
            pltpu.VMEM((rows // BLOCK, LANES, BLOCK), jnp.float32),
            pltpu.VMEM((rows // BLOCK, LANES, BLOCK), jnp.float32),
        ],
        compiler_params=pltpu.CompilerParams(vmem_limit_bytes=50 << 20),
        cost_estimate=pl.CostEstimate(
            flops=6 * rows * keys * WIDTH, bytes_accessed=4 * keys * WIDTH, transcendentals=rows * keys * HEADS
        ),
        name="attend",
    )(limit, q, k, v, sk, sv, query_frame, key_frame)


def merge_kernel(last, a_ref, a_stats_ref, b_ref, *outs):
    a_log = a_stats_ref[...]
    a_power = pltpu.roll(a_log, LANES - PART, 1)
    b_log, b_power = unpack_stats(b_ref[:, PART_WIDTH:])
    rows = a_log.shape[0]
    half = rows if last else rows // 2
    top = jnp.maximum(a_log, b_log)
    a_weight, b_weight = jnp.exp2(a_log - top), jnp.exp2(b_log - top)
    total = a_weight + b_weight
    a_share, b_share = a_weight / total, b_weight / total * (jnp.exp2(b_power) * (1.0 / STEPS))
    if not last:
        power = jnp.maximum(a_power, b_power)
        row = lax.broadcasted_iota(jnp.int32, power.shape, 0)
        steps = jnp.where(row < half, 1.0, jnp.exp2(-power) * STEPS)
        a_share, b_share = a_share * steps, b_share * steps
    for head in range(PART_HEADS):
        cols = slice(head * HEAD_DIM, (head + 1) * HEAD_DIM)
        o = a_ref[:, cols] * a_share[:, head : head + 1] + unpack(b_ref[:, cols]) * b_share[:, head : head + 1]
        outs[0][:, cols] = o[:half].astype(outs[0].dtype)
        if not last:
            outs[2][:, cols] = pack(o[half:])
    if not last:
        log_sum = jnp.maximum(top + jnp.log2(total), LOG_FLOOR)
        outs[1][...] = join_stats(log_sum[:half], power[:half])
        outs[2][:, PART_WIDTH:] = pack_stats(log_sum[half:], power[half:])


def merge(a, a_stats, b, last):
    rows = a.shape[0]
    shapes = [jax.ShapeDtypeStruct((rows, PART_WIDTH), jnp.bfloat16)] if last else halves(rows // 2)
    vmem = pl.BlockSpec(memory_space=pltpu.VMEM)
    return pl.pallas_call(
        functools.partial(merge_kernel, last),
        in_specs=[vmem] * 3,
        out_specs=[vmem] * len(shapes),
        out_shape=shapes,
        compiler_params=pltpu.CompilerParams(vmem_limit_bytes=16 << 20),
        name="merge",
    )(a, a_stats, b)


def strides(devices):
    order = []
    stride = 2
    while stride < devices:
        order.append(stride)
        stride *= 2
    if len(order) >= 2:
        order = order[1:] + order[:1]
    return order + [1]


def local(devices, queries, cache_keys, cache_values, span_keys, span_values, cache_tokens, span_start):
    me = lax.axis_index("seq")
    cache_rows, own = cache_keys.shape[0], queries.shape[0]
    order = strides(devices)

    def swap(x, stride):
        return lax.ppermute(x, "seq", [(i, i ^ stride) for i in range(devices)])

    q, holder = queries, [0]
    for stride in order:
        q = lax.optimization_barrier(jnp.concatenate([q, swap(q, stride)], axis=0))
        holder = holder + [h ^ stride for h in holder]
    position = (me ^ jnp.array(holder, jnp.int32))[:, None] * own + jnp.arange(own, dtype=jnp.int32)[None, :]
    query_frame = (span_start[0] + position.reshape(-1)) // FRAME_TOK
    query_frame = jnp.broadcast_to(query_frame[None, :], (8, devices * own))
    key_frame = (span_start[0] + me * own + jnp.arange(own, dtype=jnp.int32)) // FRAME_TOK
    key_frame = jnp.broadcast_to(key_frame[:, None], (own, LANES))
    limit = jnp.clip(cache_tokens - me * cache_rows, 0, cache_rows)
    out = attend(limit, q, cache_keys, cache_values, span_keys, span_values, query_frame, key_frame)
    held = [out[3 * group : 3 * group + 3] for group in range(GROUPS)]
    for stride in order[:0:-1]:
        held = [merge(keep, stats, swap(send, stride), False) for keep, stats, send in held]
    parts = [merge(keep, stats, swap(send, order[0]), True)[0] for keep, stats, send in held]
    return jnp.concatenate(parts, axis=1)


def solution(mesh):
    rows = P(("groups", "seq"), None)
    placed = (rows, rows, rows, rows, rows, P("groups"), P("groups"))
    return jax.shard_map(
        functools.partial(local, mesh.shape["seq"]), mesh=mesh, in_specs=placed, out_specs=rows, check_vma=False
    )
```

```python
import functools
import math

import jax
import jax.numpy as jnp
from jax import lax
from jax.experimental import pallas as pl
from jax.experimental.pallas import tpu as pltpu
from jax.sharding import PartitionSpec as P

HEAD_DIM = 128
HEADS = 20
FRAME_TOK = 1560
LANES = 128
PART = 32
NEG_FILL = -1e30
LOG_FLOOR = -30000.0
FIXED = 32768.0
HALF_RANGE = 32768
STEPS = 32512.0
PEAK_FLOOR = 1e-30
SCALE = math.log2(math.e) / math.sqrt(HEAD_DIM)
WIDTH = HEADS * HEAD_DIM
GROUPS = 2
PART_HEADS = HEADS // GROUPS
PART_WIDTH = PART_HEADS * HEAD_DIM
PAIR = 2 * HEAD_DIM
BLOCK = 128
KEY_STEP = 512
WEIGHT_STEP = 256
STAGES = (1, 4, 7)
PAD = 16
LAST = (((1,), (1,)), ((), ()))
FIRST = (((0,), (0,)), ((), ()))


def power_of(peak):
    return jnp.ceil(jnp.log2(jnp.maximum(peak, PEAK_FLOOR)))


def pack(scaled):
    return jnp.round(scaled).astype(jnp.int32).astype(jnp.int16)


def unpack(steps):
    return steps.astype(jnp.int32).astype(jnp.float32)


def pack_stats(log_sum, power):
    fixed = jnp.round(log_sum * FIXED).astype(jnp.int32)
    high = fixed // HALF_RANGE
    low = fixed - high * HALF_RANGE
    lane = lax.broadcasted_iota(jnp.int32, log_sum.shape, 1)
    packed = jnp.where(lane < PART, high, pltpu.roll(low, PART, 1))
    packed = jnp.where(lane < 2 * PART, packed, pltpu.roll(power.astype(jnp.int32), 2 * PART, 1))
    return packed.astype(jnp.int16)


def unpack_stats(packed):
    packed = packed.astype(jnp.int32)
    fixed = packed * HALF_RANGE + pltpu.roll(packed, LANES - PART, 1)
    power = pltpu.roll(packed, LANES - 2 * PART, 1)
    return fixed.astype(jnp.float32) * (1.0 / FIXED), power.astype(jnp.float32)


def attend_kernel(
    order, me_ref, tokens_hbm, start_hbm, q_ref, k_hbm, v_hbm, sk_ref, sv_ref, *refs
):
    results, refs = refs[: 3 * GROUPS], refs[3 * GROUPS :]
    k_ref, v_ref, sems, bias_ref, s_even, s_odd, top_ref, logs_ref, powers_ref, tokens_ref, start_ref, number_sems = refs
    numbers = [
        pltpu.make_async_copy(tokens_hbm, tokens_ref, number_sems.at[0]),
        pltpu.make_async_copy(start_hbm, start_ref, number_sems.at[1]),
    ]
    for copy in numbers:
        copy.start()
    rows, keys, own = q_ref.shape[0], k_ref.shape[1], sk_ref.shape[0]
    half = rows // 2
    pairs = HEADS // 2
    scores = (s_even, s_odd)
    me = me_ref[0]

    def frame_of(place):
        place = place + start_ref[0]
        last = (FRAME_TOK + rows - 2) // FRAME_TOK
        return sum((place >= number * FRAME_TOK).astype(jnp.int32) for number in range(1, last + 1))

    def copy_of(pair, which):
        cols = pl.ds(pair * PAIR, PAIR)
        source, target = ((k_hbm, k_ref), (v_hbm, v_ref))[which]
        return pltpu.make_async_copy(source.at[:, cols], target.at[pair], sems.at[pair, which])

    for pair in range(pairs):
        copy_of(pair, 0).start()
        copy_of(pair, 1).start()
    logs_ref[...] = jnp.zeros_like(logs_ref)
    powers_ref[...] = jnp.zeros_like(powers_ref)
    for copy in numbers:
        copy.wait()
    slot = lax.broadcasted_iota(jnp.int32, bias_ref.shape, 0)
    bias_ref[...] = jnp.where(slot < tokens_ref[0] - me * keys, 0.0, NEG_FILL)
    pad = jnp.zeros((PAD - own, PAIR), jnp.bfloat16)

    def block_at(block):
        first = block * BLOCK if rows == BLOCK else pl.multiple_of(block * BLOCK, BLOCK)
        block_rows = pl.ds(first, BLOCK)
        row = first + lax.broadcasted_iota(jnp.int32, (own, BLOCK), 1)
        device, owner = row // own, me
        for bit, stride in enumerate(order):
            owner = owner ^ (((device >> bit) & 1) * stride)
        query_frame = frame_of(owner * own + row - device * own)
        key_frame = frame_of(me * own + lax.broadcasted_iota(jnp.int32, (own, BLOCK), 0))
        span_bias = jnp.where(key_frame <= query_frame, 0.0, NEG_FILL)
        span_bias = jnp.concatenate([span_bias, span_bias], axis=1)

        def columns(pair):
            return slice(pair * PAIR, (pair + 1) * PAIR)

        def score(pair, slot):
            cols = columns(pair)
            q = q_ref[block_rows, cols]
            zero = jnp.zeros((BLOCK, HEAD_DIM), q.dtype)
            q = jnp.concatenate(
                [jnp.concatenate([q[:, :HEAD_DIM], zero], 1), jnp.concatenate([zero, q[:, HEAD_DIM:]], 1)], 0
            )
            s2 = lax.dot_general(sk_ref[:, cols], q, LAST, preferred_element_type=jnp.float32) + span_bias
            scores[slot][keys:, :] = s2
            tops = s2
            for chunk in range(0, keys, KEY_STEP):
                part = pl.ds(chunk, KEY_STEP)
                s = lax.dot_general(k_ref[pair, part, :], q, LAST, preferred_element_type=jnp.float32)
                bias = bias_ref[part, :]
                s = s + jnp.concatenate([bias, bias], axis=1)
                scores[slot][part, :] = s
                tops = jnp.maximum(tops, jnp.max(s.reshape(KEY_STEP // 8, 8, PAIR), axis=0))
                yield
            top_ref[slot : slot + 1, :] = jnp.max(tops, axis=0, keepdims=True)

        def weigh(pair, head, slot, beside, finish):
            cols = columns(pair)
            lanes = slice(head * HEAD_DIM, (head + 1) * HEAD_DIM)
            top = top_ref[slot : slot + 1, lanes]
            total = jnp.zeros((8, HEAD_DIM), jnp.float32)
            parts = []
            for chunk in list(range(0, keys, WEIGHT_STEP)) + [keys]:
                size = WEIGHT_STEP if chunk < keys else own
                if chunk < keys:
                    next(beside, None)
                    next(finish, None)
                p = jnp.exp2((scores[slot][chunk : chunk + size, lanes] - top) * SCALE)
                total = total + jnp.sum(p.reshape(size // 8, 8, HEAD_DIM), axis=0)
                high = p.astype(jnp.bfloat16)
                low = (p - high.astype(jnp.float32)).astype(jnp.bfloat16)
                parts.append(jnp.concatenate([high, low], axis=1))
            for _ in finish:
                pass
            sv = jnp.concatenate([sv_ref[:, cols], pad], 0)
            both = lax.dot_general(
                v_ref[pair, :, lanes], jnp.concatenate(parts[:-1], 0), FIRST, preferred_element_type=jnp.float32
            ) + lax.dot_general(
                sv[:, lanes], jnp.concatenate([parts[-1], pad], 0), FIRST, preferred_element_type=jnp.float32
            )
            return both, jnp.sum(total, axis=0, keepdims=True), top

        def place(pair, head, both, total, top):
            group, within = divmod(pair * 2 + head, PART_HEADS)
            cols = slice(within * HEAD_DIM, (within + 1) * HEAD_DIM)
            keep_ref, _, send_ref = results[3 * group : 3 * group + 3]
            o = (both[:, :HEAD_DIM] + both[:, HEAD_DIM:]) * (1.0 / total)
            power = power_of(jnp.max(jnp.abs(o), axis=0, keepdims=True))
            steps = jnp.exp2(-power) * STEPS
            lane = lax.broadcasted_iota(jnp.int32, steps.shape, 1)
            steps = jnp.where(first + lane < half, 1.0, steps)
            number = group * (LANES // GROUPS) + within
            logs_ref[block, number : number + 1, :] = jnp.maximum(top * SCALE + jnp.log2(total), LOG_FLOOR)
            powers_ref[block, number : number + 1, :] = power
            yield
            o = jnp.transpose(o * steps)
            yield
            if rows == BLOCK:
                keep_ref[:, cols] = o[:half]
                send_ref[:, cols] = pack(o[half:])
            else:
                @pl.when(first < half)
                def _():
                    keep_ref[block_rows, cols] = o

                @pl.when(first >= half)
                def _():
                    send_ref[pl.ds(pl.multiple_of(first - half, BLOCK), BLOCK), cols] = pack(o)

        def arrive(key_pairs, value_pairs):
            def wait():
                for pair in key_pairs:
                    if pair < pairs:
                        copy_of(pair, 0).wait()
                for pair in value_pairs:
                    copy_of(pair, 1).wait()

            wait() if rows == BLOCK else pl.when(block == 0)(wait)

        finish = iter(())
        arrive([0], [])
        for _ in score(0, 0):
            pass
        arrive([1], [0])
        for pair in range(pairs):
            if pair in STAGES:
                until = min([p for p in STAGES if p > pair] + [pairs])
                arrive(range(pair + 1, until + 1), range(pair, until))
            beside = score(pair + 1, (pair + 1) % 2) if pair + 1 < pairs else iter(())
            for head in range(2):
                done = weigh(pair, head, pair % 2, beside, finish)
                finish = place(pair, head, *done)
            for _ in beside:
                pass
        for _ in finish:
            pass

    if rows == BLOCK:
        block_at(0)
    else:
        pl.loop(0, rows // BLOCK)(block_at)
    for block in range(rows // BLOCK):
        logs, powers = jnp.transpose(logs_ref[block]), jnp.transpose(powers_ref[block])
        here = slice(block * BLOCK, min((block + 1) * BLOCK, half))
        kept = max(here.stop - here.start, 0)
        for group in range(GROUPS):
            _, keep_stats_ref, send_ref = results[3 * group : 3 * group + 3]
            if group:
                logs, powers = (pltpu.roll(x, LANES - LANES // GROUPS, 1) for x in (logs, powers))
            if kept:
                keep_stats_ref[here, :] = join_stats(logs[:kept], powers[:kept])
            if kept < BLOCK:
                there = slice(block * BLOCK + kept - half, (block + 1) * BLOCK - half)
                send_ref[there, PART_WIDTH:] = pack_stats(logs[kept:], powers[kept:])


def join_stats(log_sum, power):
    lane = lax.broadcasted_iota(jnp.int32, log_sum.shape, 1)
    return jnp.where(lane < PART, log_sum, pltpu.roll(power, PART, 1))


def halves(rows):
    return [
        jax.ShapeDtypeStruct((rows, PART_WIDTH), jnp.float32),
        jax.ShapeDtypeStruct((rows, LANES), jnp.float32),
        jax.ShapeDtypeStruct((rows, PART_WIDTH + LANES), jnp.int16),
    ]


def attend(order, me, tokens, start, q, k, v, sk, sv):
    vmem = pl.BlockSpec(memory_space=pltpu.VMEM)
    hbm = pl.BlockSpec(memory_space=pltpu.HBM)
    rows, keys, own = q.shape[0], k.shape[0], sk.shape[0]
    pairs = HEADS // 2
    return pl.pallas_call(
        functools.partial(attend_kernel, order),
        in_specs=[pl.BlockSpec(memory_space=pltpu.SMEM), hbm, hbm, vmem, hbm, hbm, vmem, vmem],
        out_specs=[vmem] * (3 * GROUPS),
        out_shape=halves(rows // 2) * GROUPS,
        scratch_shapes=[
            pltpu.VMEM((pairs, keys, PAIR), k.dtype),
            pltpu.VMEM((pairs, keys, PAIR), v.dtype),
            pltpu.SemaphoreType.DMA((pairs, 2)),
            pltpu.VMEM((keys, LANES), jnp.float32),
            pltpu.VMEM((keys + own, PAIR), jnp.float32),
            pltpu.VMEM((keys + own, PAIR), jnp.float32),
            pltpu.VMEM((8, PAIR), jnp.float32),
            pltpu.VMEM((rows // BLOCK, LANES, BLOCK), jnp.float32),
            pltpu.VMEM((rows // BLOCK, LANES, BLOCK), jnp.float32),
            pltpu.SMEM((1,), jnp.int32),
            pltpu.SMEM((1,), jnp.int32),
            pltpu.SemaphoreType.DMA((2,)),
        ],
        compiler_params=pltpu.CompilerParams(vmem_limit_bytes=50 << 20),
        cost_estimate=pl.CostEstimate(
            flops=6 * rows * keys * WIDTH, bytes_accessed=4 * keys * WIDTH, transcendentals=rows * keys * HEADS
        ),
        name="attend",
    )(me.reshape(1), tokens, start, q, k, v, sk, sv)


def merge_kernel(last, a_ref, a_stats_ref, b_ref, *outs):
    a_log = a_stats_ref[...]
    a_power = pltpu.roll(a_log, LANES - PART, 1)
    b_log, b_power = unpack_stats(b_ref[:, PART_WIDTH:])
    rows = a_log.shape[0]
    half = rows if last else rows // 2
    top = jnp.maximum(a_log, b_log)
    a_weight, b_weight = jnp.exp2(a_log - top), jnp.exp2(b_log - top)
    total = a_weight + b_weight
    a_share, b_share = a_weight / total, b_weight / total * (jnp.exp2(b_power) * (1.0 / STEPS))
    if not last:
        power = jnp.maximum(a_power, b_power)
        row = lax.broadcasted_iota(jnp.int32, power.shape, 0)
        steps = jnp.where(row < half, 1.0, jnp.exp2(-power) * STEPS)
        a_share, b_share = a_share * steps, b_share * steps
    for head in range(PART_HEADS):
        cols = slice(head * HEAD_DIM, (head + 1) * HEAD_DIM)
        o = a_ref[:, cols] * a_share[:, head : head + 1] + unpack(b_ref[:, cols]) * b_share[:, head : head + 1]
        outs[0][:, cols] = o[:half].astype(outs[0].dtype)
        if not last:
            outs[2][:, cols] = pack(o[half:])
    if not last:
        log_sum = jnp.maximum(top + jnp.log2(total), LOG_FLOOR)
        outs[1][...] = join_stats(log_sum[:half], power[:half])
        outs[2][:, PART_WIDTH:] = pack_stats(log_sum[half:], power[half:])


def merge(a, a_stats, b, last):
    rows = a.shape[0]
    shapes = [jax.ShapeDtypeStruct((rows, PART_WIDTH), jnp.bfloat16)] if last else halves(rows // 2)
    vmem = pl.BlockSpec(memory_space=pltpu.VMEM)
    return pl.pallas_call(
        functools.partial(merge_kernel, last),
        in_specs=[vmem] * 3,
        out_specs=[vmem] * len(shapes),
        out_shape=shapes,
        compiler_params=pltpu.CompilerParams(vmem_limit_bytes=16 << 20),
        name="merge",
    )(a, a_stats, b)


def strides(devices):
    order = []
    stride = 2
    while stride < devices:
        order.append(stride)
        stride *= 2
    if len(order) >= 2:
        order = order[1:] + order[:1]
    return order + [1]


def local(devices, queries, cache_keys, cache_values, span_keys, span_values, cache_tokens, span_start):
    order = strides(devices)

    def swap(x, stride):
        return lax.ppermute(x, "seq", [(i, i ^ stride) for i in range(devices)])

    def stack(pieces):
        return lax.optimization_barrier(jnp.concatenate(pieces, axis=0))

    early, late = [], [queries]
    for stride in order:
        got = [swap(piece, stride) for piece in early + late]
        early, late = [stack(early + late) if early else late[0]], [stack(got) if len(got) > 1 else got[0]]
    q = stack(early + late)
    out = attend(
        tuple(order), lax.axis_index("seq"), cache_tokens, span_start, q, cache_keys, cache_values, span_keys, span_values
    )
    held = [out[3 * group : 3 * group + 3] for group in range(GROUPS)]
    for stride in order[:0:-1]:
        held = [merge(keep, stats, swap(send, stride), False) for keep, stats, send in held]
    parts = [merge(keep, stats, swap(send, order[0]), True)[0] for keep, stats, send in held]
    return jnp.concatenate(parts, axis=1)


def solution(mesh):
    rows = P(("groups", "seq"), None)
    placed = (rows, rows, rows, rows, rows, P("groups"), P("groups"))
    return jax.shard_map(
        functools.partial(local, mesh.shape["seq"]), mesh=mesh, in_specs=placed, out_specs=rows, check_vma=False
    )
```

```python
import functools
import math

import jax
import jax.numpy as jnp
from jax import lax
from jax.experimental import pallas as pl
from jax.experimental.pallas import tpu as pltpu
from jax.sharding import PartitionSpec as P

HEAD_DIM = 128
HEADS = 20
FRAME_TOK = 1560
LANES = 128
PART = 32
NEG_FILL = -1e30
LOG_FLOOR = -30000.0
FIXED = 32768.0
HALF_RANGE = 32768
STEPS = 32512.0
PEAK_FLOOR = 1e-30
SCALE = math.log2(math.e) / math.sqrt(HEAD_DIM)
WIDTH = HEADS * HEAD_DIM
GROUPS = 2
PART_HEADS = HEADS // GROUPS
PART_WIDTH = PART_HEADS * HEAD_DIM
PAIR = 2 * HEAD_DIM
BLOCK = 128
WEIGHT_STEP = 256
STAGES = (1, 4, 7)
PAD = 16
LAST = (((1,), (1,)), ((), ()))
FIRST = (((0,), (0,)), ((), ()))


def power_of(peak):
    return jnp.ceil(jnp.log2(jnp.maximum(peak, PEAK_FLOOR)))


def pack(scaled):
    return jnp.round(scaled).astype(jnp.int32).astype(jnp.int16)


def unpack(steps):
    return steps.astype(jnp.int32).astype(jnp.float32)


def pack_stats(log_sum, power):
    fixed = jnp.round(log_sum * FIXED).astype(jnp.int32)
    high = fixed // HALF_RANGE
    low = fixed - high * HALF_RANGE
    lane = lax.broadcasted_iota(jnp.int32, log_sum.shape, 1)
    packed = jnp.where(lane < PART, high, pltpu.roll(low, PART, 1))
    packed = jnp.where(lane < 2 * PART, packed, pltpu.roll(power.astype(jnp.int32), 2 * PART, 1))
    return packed.astype(jnp.int16)


def unpack_stats(packed):
    packed = packed.astype(jnp.int32)
    fixed = packed * HALF_RANGE + pltpu.roll(packed, LANES - PART, 1)
    power = pltpu.roll(packed, LANES - 2 * PART, 1)
    return fixed.astype(jnp.float32) * (1.0 / FIXED), power.astype(jnp.float32)


def attend_kernel(
    order, me_ref, tokens_hbm, start_hbm, q_ref, k_hbm, v_hbm, sk_ref, sv_ref, *refs
):
    results, refs = refs[: 3 * GROUPS], refs[3 * GROUPS :]
    k_ref, v_ref, sems, bias_ref, s_even, s_odd, top_ref, logs_ref, powers_ref, tokens_ref, start_ref, number_sems = refs
    numbers = [
        pltpu.make_async_copy(tokens_hbm, tokens_ref, number_sems.at[0]),
        pltpu.make_async_copy(start_hbm, start_ref, number_sems.at[1]),
    ]
    for copy in numbers:
        copy.start()
    rows, keys, own = q_ref.shape[0], k_ref.shape[1], sk_ref.shape[0]
    half = rows // 2
    pairs = HEADS // 2
    scores = (s_even, s_odd)
    me = me_ref[0]

    def frame_of(place):
        place = place + start_ref[0]
        last = (FRAME_TOK + rows - 2) // FRAME_TOK
        return sum((place >= number * FRAME_TOK).astype(jnp.int32) for number in range(1, last + 1))

    def copy_of(pair, which):
        cols = pl.ds(pair * PAIR, PAIR)
        source, target = ((k_hbm, k_ref), (v_hbm, v_ref))[which]
        return pltpu.make_async_copy(source.at[:, cols], target.at[pair], sems.at[pair, which])

    for pair in range(pairs):
        copy_of(pair, 0).start()
        copy_of(pair, 1).start()
    logs_ref[...] = jnp.zeros_like(logs_ref)
    powers_ref[...] = jnp.zeros_like(powers_ref)
    for copy in numbers:
        copy.wait()
    slot = lax.broadcasted_iota(jnp.int32, bias_ref.shape, 0)
    bias_ref[...] = jnp.where(slot < tokens_ref[0] - me * keys, 0.0, NEG_FILL)
    pad = jnp.zeros((PAD - own, PAIR), jnp.bfloat16)

    def block_at(block):
        first = block * BLOCK if rows == BLOCK else pl.multiple_of(block * BLOCK, BLOCK)
        block_rows = pl.ds(first, BLOCK)
        row = first + lax.broadcasted_iota(jnp.int32, (own, BLOCK), 1)
        device, owner = row // own, me
        for bit, stride in enumerate(order):
            owner = owner ^ (((device >> bit) & 1) * stride)
        query_frame = frame_of(owner * own + row - device * own)
        key_frame = frame_of(me * own + lax.broadcasted_iota(jnp.int32, (own, BLOCK), 0))
        span_bias = jnp.where(key_frame <= query_frame, 0.0, NEG_FILL)
        span_bias = jnp.concatenate([span_bias, span_bias], axis=1)

        def columns(pair):
            return slice(pair * PAIR, (pair + 1) * PAIR)

        def score(pair, slot):
            cols = columns(pair)
            q = q_ref[block_rows, cols]
            zero = jnp.zeros((BLOCK, HEAD_DIM), q.dtype)
            q = jnp.concatenate(
                [jnp.concatenate([q[:, :HEAD_DIM], zero], 1), jnp.concatenate([zero, q[:, HEAD_DIM:]], 1)], 0
            )
            s2 = lax.dot_general(sk_ref[:, cols], q, LAST, preferred_element_type=jnp.float32) + span_bias
            scores[slot][keys:, :] = s2
            tops = s2
            s = lax.dot_general(k_ref[pair], q, LAST, preferred_element_type=jnp.float32)
            bias = bias_ref[...]
            s = s + jnp.concatenate([bias, bias], axis=1)
            scores[slot][:keys, :] = s
            tops = jnp.maximum(tops, jnp.max(s.reshape(keys // 8, 8, PAIR), axis=0))
            yield
            top_ref[slot : slot + 1, :] = jnp.max(tops, axis=0, keepdims=True)

        def weigh(pair, head, slot, beside, finish):
            cols = columns(pair)
            lanes = slice(head * HEAD_DIM, (head + 1) * HEAD_DIM)
            top = top_ref[slot : slot + 1, lanes]
            total = jnp.zeros((8, HEAD_DIM), jnp.float32)
            parts = []
            for chunk in list(range(0, keys, WEIGHT_STEP)) + [keys]:
                size = WEIGHT_STEP if chunk < keys else own
                if chunk < keys:
                    next(beside, None)
                    next(finish, None)
                p = jnp.exp2((scores[slot][chunk : chunk + size, lanes] - top) * SCALE)
                total = total + jnp.sum(p.reshape(size // 8, 8, HEAD_DIM), axis=0)
                high = p.astype(jnp.bfloat16)
                low = (p - high.astype(jnp.float32)).astype(jnp.bfloat16)
                parts.append(jnp.concatenate([high, low], axis=1))
            for _ in finish:
                pass
            sv = jnp.concatenate([sv_ref[:, cols], pad], 0)
            both = lax.dot_general(
                v_ref[pair, :, lanes], jnp.concatenate(parts[:-1], 0), FIRST, preferred_element_type=jnp.float32
            ) + lax.dot_general(
                sv[:, lanes], jnp.concatenate([parts[-1], pad], 0), FIRST, preferred_element_type=jnp.float32
            )
            return both, jnp.sum(total, axis=0, keepdims=True), top

        def place(pair, head, both, total, top):
            group, within = divmod(pair * 2 + head, PART_HEADS)
            cols = slice(within * HEAD_DIM, (within + 1) * HEAD_DIM)
            keep_ref, _, send_ref = results[3 * group : 3 * group + 3]
            o = (both[:, :HEAD_DIM] + both[:, HEAD_DIM:]) * (1.0 / total)
            power = power_of(jnp.max(jnp.abs(o), axis=0, keepdims=True))
            steps = jnp.exp2(-power) * STEPS
            lane = lax.broadcasted_iota(jnp.int32, steps.shape, 1)
            steps = jnp.where(first + lane < half, 1.0, steps)
            number = group * (LANES // GROUPS) + within
            logs_ref[block, number : number + 1, :] = jnp.maximum(top * SCALE + jnp.log2(total), LOG_FLOOR)
            powers_ref[block, number : number + 1, :] = power
            yield
            o = jnp.transpose(o * steps)
            yield
            if rows == BLOCK:
                keep_ref[:, cols] = o[:half]
                send_ref[:, cols] = pack(o[half:])
            else:
                @pl.when(first < half)
                def _():
                    keep_ref[block_rows, cols] = o

                @pl.when(first >= half)
                def _():
                    send_ref[pl.ds(pl.multiple_of(first - half, BLOCK), BLOCK), cols] = pack(o)

        def arrive(key_pairs, value_pairs):
            def wait():
                for pair in key_pairs:
                    if pair < pairs:
                        copy_of(pair, 0).wait()
                for pair in value_pairs:
                    copy_of(pair, 1).wait()

            wait() if rows == BLOCK else pl.when(block == 0)(wait)

        finish = iter(())
        arrive([0], [])
        for _ in score(0, 0):
            pass
        arrive([1], [0])
        for pair in range(pairs):
            if pair in STAGES:
                until = min([p for p in STAGES if p > pair] + [pairs])
                arrive(range(pair + 1, until + 1), range(pair, until))
            beside = score(pair + 1, (pair + 1) % 2) if pair + 1 < pairs else iter(())
            for head in range(2):
                done = weigh(pair, head, pair % 2, beside, finish)
                finish = place(pair, head, *done)
            for _ in beside:
                pass
        for _ in finish:
            pass

    if rows == BLOCK:
        block_at(0)
    else:
        pl.loop(0, rows // BLOCK)(block_at)
    for block in range(rows // BLOCK):
        logs, powers = jnp.transpose(logs_ref[block]), jnp.transpose(powers_ref[block])
        here = slice(block * BLOCK, min((block + 1) * BLOCK, half))
        kept = max(here.stop - here.start, 0)
        for group in range(GROUPS):
            _, keep_stats_ref, send_ref = results[3 * group : 3 * group + 3]
            if group:
                logs, powers = (pltpu.roll(x, LANES - LANES // GROUPS, 1) for x in (logs, powers))
            if kept:
                keep_stats_ref[here, :] = join_stats(logs[:kept], powers[:kept])
            if kept < BLOCK:
                there = slice(block * BLOCK + kept - half, (block + 1) * BLOCK - half)
                send_ref[there, PART_WIDTH:] = pack_stats(logs[kept:], powers[kept:])


def join_stats(log_sum, power):
    lane = lax.broadcasted_iota(jnp.int32, log_sum.shape, 1)
    return jnp.where(lane < PART, log_sum, pltpu.roll(power, PART, 1))


def halves(rows):
    return [
        jax.ShapeDtypeStruct((rows, PART_WIDTH), jnp.float32),
        jax.ShapeDtypeStruct((rows, LANES), jnp.float32),
        jax.ShapeDtypeStruct((rows, PART_WIDTH + LANES), jnp.int16),
    ]


def attend(order, me, tokens, start, q, k, v, sk, sv):
    vmem = pl.BlockSpec(memory_space=pltpu.VMEM)
    hbm = pl.BlockSpec(memory_space=pltpu.HBM)
    rows, keys, own = q.shape[0], k.shape[0], sk.shape[0]
    pairs = HEADS // 2
    return pl.pallas_call(
        functools.partial(attend_kernel, order),
        in_specs=[pl.BlockSpec(memory_space=pltpu.SMEM), hbm, hbm, vmem, hbm, hbm, vmem, vmem],
        out_specs=[vmem] * (3 * GROUPS),
        out_shape=halves(rows // 2) * GROUPS,
        scratch_shapes=[
            pltpu.VMEM((pairs, keys, PAIR), k.dtype),
            pltpu.VMEM((pairs, keys, PAIR), v.dtype),
            pltpu.SemaphoreType.DMA((pairs, 2)),
            pltpu.VMEM((keys, LANES), jnp.float32),
            pltpu.VMEM((keys + own, PAIR), jnp.float32),
            pltpu.VMEM((keys + own, PAIR), jnp.float32),
            pltpu.VMEM((8, PAIR), jnp.float32),
            pltpu.VMEM((rows // BLOCK, LANES, BLOCK), jnp.float32),
            pltpu.VMEM((rows // BLOCK, LANES, BLOCK), jnp.float32),
            pltpu.SMEM((1,), jnp.int32),
            pltpu.SMEM((1,), jnp.int32),
            pltpu.SemaphoreType.DMA((2,)),
        ],
        compiler_params=pltpu.CompilerParams(vmem_limit_bytes=50 << 20),
        cost_estimate=pl.CostEstimate(
            flops=6 * rows * keys * WIDTH, bytes_accessed=4 * keys * WIDTH, transcendentals=rows * keys * HEADS
        ),
        name="attend",
    )(me.reshape(1), tokens, start, q, k, v, sk, sv)


def merge_kernel(last, a_ref, a_stats_ref, b_ref, *outs):
    a_log = a_stats_ref[...]
    a_power = pltpu.roll(a_log, LANES - PART, 1)
    b_log, b_power = unpack_stats(b_ref[:, PART_WIDTH:])
    rows = a_log.shape[0]
    half = rows if last else rows // 2
    top = jnp.maximum(a_log, b_log)
    a_weight, b_weight = jnp.exp2(a_log - top), jnp.exp2(b_log - top)
    total = a_weight + b_weight
    a_share, b_share = a_weight / total, b_weight / total * (jnp.exp2(b_power) * (1.0 / STEPS))
    if not last:
        power = jnp.maximum(a_power, b_power)
        row = lax.broadcasted_iota(jnp.int32, power.shape, 0)
        steps = jnp.where(row < half, 1.0, jnp.exp2(-power) * STEPS)
        a_share, b_share = a_share * steps, b_share * steps
    for head in range(PART_HEADS):
        cols = slice(head * HEAD_DIM, (head + 1) * HEAD_DIM)
        o = a_ref[:, cols] * a_share[:, head : head + 1] + unpack(b_ref[:, cols]) * b_share[:, head : head + 1]
        outs[0][:, cols] = o[:half].astype(outs[0].dtype)
        if not last:
            outs[2][:, cols] = pack(o[half:])
    if not last:
        log_sum = jnp.maximum(top + jnp.log2(total), LOG_FLOOR)
        outs[1][...] = join_stats(log_sum[:half], power[:half])
        outs[2][:, PART_WIDTH:] = pack_stats(log_sum[half:], power[half:])


def merge(a, a_stats, b, last):
    rows = a.shape[0]
    shapes = [jax.ShapeDtypeStruct((rows, PART_WIDTH), jnp.bfloat16)] if last else halves(rows // 2)
    vmem = pl.BlockSpec(memory_space=pltpu.VMEM)
    return pl.pallas_call(
        functools.partial(merge_kernel, last),
        in_specs=[vmem] * 3,
        out_specs=[vmem] * len(shapes),
        out_shape=shapes,
        compiler_params=pltpu.CompilerParams(vmem_limit_bytes=16 << 20),
        name="merge",
    )(a, a_stats, b)


def strides(devices):
    order = []
    stride = 2
    while stride < devices:
        order.append(stride)
        stride *= 2
    if len(order) >= 2:
        order = order[1:] + order[:1]
    return order + [1]


def local(devices, queries, cache_keys, cache_values, span_keys, span_values, cache_tokens, span_start):
    order = strides(devices)

    def swap(x, stride):
        return lax.ppermute(x, "seq", [(i, i ^ stride) for i in range(devices)])

    def stack(pieces):
        return lax.optimization_barrier(jnp.concatenate(pieces, axis=0))

    early, late = [], [queries]
    for stride in order:
        got = [swap(piece, stride) for piece in early + late]
        early, late = [stack(early + late) if early else late[0]], [stack(got) if len(got) > 1 else got[0]]
    q = stack(early + late)
    out = attend(
        tuple(order), lax.axis_index("seq"), cache_tokens, span_start, q, cache_keys, cache_values, span_keys, span_values
    )
    held = [out[3 * group : 3 * group + 3] for group in range(GROUPS)]
    for stride in order[:0:-1]:
        held = [merge(keep, stats, swap(send, stride), False) for keep, stats, send in held]
    parts = [merge(keep, stats, swap(send, order[0]), True)[0] for keep, stats, send in held]
    return jnp.concatenate(parts, axis=1)


def solution(mesh):
    rows = P(("groups", "seq"), None)
    placed = (rows, rows, rows, rows, rows, P("groups"), P("groups"))
    return jax.shard_map(
        functools.partial(local, mesh.shape["seq"]), mesh=mesh, in_specs=placed, out_specs=rows, check_vma=False
    )
```

```python
import functools
import math

import jax
import jax.numpy as jnp
from jax import lax
from jax.experimental import pallas as pl
from jax.experimental.pallas import tpu as pltpu
from jax.sharding import PartitionSpec as P

HEAD_DIM = 128
HEADS = 20
FRAME_TOK = 1560
LANES = 128
PART = 32
NEG_FILL = -1e30
LOG_FLOOR = -30000.0
FIXED = 32768.0
HALF_RANGE = 32768
STEPS = 32512.0
PEAK_FLOOR = 1e-30
SCALE = math.log2(math.e) / math.sqrt(HEAD_DIM)
WIDTH = HEADS * HEAD_DIM
GROUPS = 2
PART_HEADS = HEADS // GROUPS
PART_WIDTH = PART_HEADS * HEAD_DIM
PAIR = 2 * HEAD_DIM
BLOCK = 128
WEIGHT_STEP = 256
STAGES = (1, 4, 7)
PAD = 16
LAST = (((1,), (1,)), ((), ()))
FIRST = (((0,), (0,)), ((), ()))


def power_of(peak):
    return jnp.ceil(jnp.log2(jnp.maximum(peak, PEAK_FLOOR)))


def pack(scaled):
    return jnp.round(scaled).astype(jnp.int32).astype(jnp.int16)


def unpack(steps):
    return steps.astype(jnp.int32).astype(jnp.float32)


def pack_stats(log_sum, power):
    fixed = jnp.round(log_sum * FIXED).astype(jnp.int32)
    high = fixed // HALF_RANGE
    low = fixed - high * HALF_RANGE
    lane = lax.broadcasted_iota(jnp.int32, log_sum.shape, 1)
    packed = jnp.where(lane < PART, high, pltpu.roll(low, PART, 1))
    packed = jnp.where(lane < 2 * PART, packed, pltpu.roll(power.astype(jnp.int32), 2 * PART, 1))
    return packed.astype(jnp.int16)


def unpack_stats(packed):
    packed = packed.astype(jnp.int32)
    fixed = packed * HALF_RANGE + pltpu.roll(packed, LANES - PART, 1)
    power = pltpu.roll(packed, LANES - 2 * PART, 1)
    return fixed.astype(jnp.float32) * (1.0 / FIXED), power.astype(jnp.float32)


def attend_kernel(
    order, me_ref, tokens_hbm, start_hbm, q_ref, k_hbm, v_hbm, sk_ref, sv_ref, *refs
):
    results, refs = refs[: 3 * GROUPS], refs[3 * GROUPS :]
    k_ref, v_ref, sems, bias_ref, s_even, s_odd, top_ref, logs_ref, powers_ref, tokens_ref, start_ref, number_sems = refs
    numbers = [
        pltpu.make_async_copy(tokens_hbm, tokens_ref, number_sems.at[0]),
        pltpu.make_async_copy(start_hbm, start_ref, number_sems.at[1]),
    ]
    for copy in numbers:
        copy.start()
    rows, keys, own = q_ref.shape[0], k_ref.shape[1], sk_ref.shape[0]
    half = rows // 2
    pairs = HEADS // 2
    scores = (s_even, s_odd)
    me = me_ref[0]

    def frame_of(place):
        place = place + start_ref[0]
        last = (FRAME_TOK + rows - 2) // FRAME_TOK
        return sum((place >= number * FRAME_TOK).astype(jnp.int32) for number in range(1, last + 1))

    def copy_of(pair, which):
        cols = pl.ds(pair * PAIR, PAIR)
        source, target = ((k_hbm, k_ref), (v_hbm, v_ref))[which]
        return pltpu.make_async_copy(source.at[:, cols], target.at[pair], sems.at[pair, which])

    for pair in range(pairs):
        copy_of(pair, 0).start()
        copy_of(pair, 1).start()
    logs_ref[...] = jnp.zeros_like(logs_ref)
    powers_ref[...] = jnp.zeros_like(powers_ref)
    for copy in numbers:
        copy.wait()
    slot = lax.broadcasted_iota(jnp.int32, bias_ref.shape, 0)
    bias_ref[...] = jnp.where(slot < tokens_ref[0] - me * keys, 0.0, NEG_FILL)
    pad = jnp.zeros((PAD - own, PAIR), jnp.bfloat16)

    def block_at(block):
        first = block * BLOCK if rows == BLOCK else pl.multiple_of(block * BLOCK, BLOCK)
        block_rows = pl.ds(first, BLOCK)
        row = first + lax.broadcasted_iota(jnp.int32, (own, BLOCK), 1)
        device, owner = row // own, me
        for bit, stride in enumerate(order):
            owner = owner ^ (((device >> bit) & 1) * stride)
        query_frame = frame_of(owner * own + row - device * own)
        key_frame = frame_of(me * own + lax.broadcasted_iota(jnp.int32, (own, BLOCK), 0))
        span_bias = jnp.where(key_frame <= query_frame, 0.0, NEG_FILL)
        span_bias = jnp.concatenate([span_bias, span_bias], axis=1)

        def columns(pair):
            return slice(pair * PAIR, (pair + 1) * PAIR)

        def score(pair, slot):
            cols = columns(pair)
            q = q_ref[block_rows, cols]
            zero = jnp.zeros((BLOCK, HEAD_DIM), q.dtype)
            q = jnp.concatenate(
                [jnp.concatenate([q[:, :HEAD_DIM], zero], 1), jnp.concatenate([zero, q[:, HEAD_DIM:]], 1)], 0
            )
            s2 = lax.dot_general(sk_ref[:, cols], q, LAST, preferred_element_type=jnp.float32) + span_bias
            scores[slot][keys:, :] = s2
            tops = s2
            s = lax.dot_general(k_ref[pair], q, LAST, preferred_element_type=jnp.float32)
            bias = bias_ref[...]
            s = s + jnp.concatenate([bias, bias], axis=1)
            scores[slot][:keys, :] = s
            tops = jnp.maximum(tops, jnp.max(s.reshape(keys // 8, 8, PAIR), axis=0))
            yield
            top_ref[slot : slot + 1, :] = jnp.max(tops, axis=0, keepdims=True)

        def weigh(pair, head, slot, beside, finish):
            cols = columns(pair)
            lanes = slice(head * HEAD_DIM, (head + 1) * HEAD_DIM)
            top = top_ref[slot : slot + 1, lanes]
            total = jnp.zeros((8, HEAD_DIM), jnp.float32)
            parts = []
            for chunk in list(range(0, keys, WEIGHT_STEP)) + [keys]:
                size = WEIGHT_STEP if chunk < keys else own
                if chunk < keys:
                    next(beside, None)
                    next(finish, None)
                p = jnp.exp2((scores[slot][chunk : chunk + size, lanes] - top) * SCALE)
                total = total + jnp.sum(p.reshape(size // 8, 8, HEAD_DIM), axis=0)
                high = p.astype(jnp.bfloat16)
                low = (p - high.astype(jnp.float32)).astype(jnp.bfloat16)
                parts.append(jnp.concatenate([high, low], axis=1))
            for _ in finish:
                pass
            sv = jnp.concatenate([sv_ref[:, cols], pad], 0)
            both = lax.dot_general(
                v_ref[pair, :, lanes], jnp.concatenate(parts[:-1], 0), FIRST, preferred_element_type=jnp.float32
            ) + lax.dot_general(
                sv[:, lanes], jnp.concatenate([parts[-1], pad], 0), FIRST, preferred_element_type=jnp.float32
            )
            return both, jnp.sum(total, axis=0, keepdims=True), top

        def place(pair, head, both, total, top):
            group, within = divmod(pair * 2 + head, PART_HEADS)
            cols = slice(within * HEAD_DIM, (within + 1) * HEAD_DIM)
            keep_ref, _, send_ref = results[3 * group : 3 * group + 3]
            o = (both[:, :HEAD_DIM] + both[:, HEAD_DIM:]) * (1.0 / total)
            power = power_of(jnp.max(jnp.abs(o), axis=0, keepdims=True))
            steps = jnp.exp2(-power) * STEPS
            lane = lax.broadcasted_iota(jnp.int32, steps.shape, 1)
            steps = jnp.where(first + lane < half, 1.0, steps)
            number = group * (LANES // GROUPS) + within
            logs_ref[block, number : number + 1, :] = jnp.maximum(top * SCALE + jnp.log2(total), LOG_FLOOR)
            powers_ref[block, number : number + 1, :] = power
            yield
            o = jnp.transpose(o * steps)
            yield
            if rows == BLOCK:
                keep_ref[:, cols] = o[:half]
                send_ref[:, cols] = pack(o[half:])
            else:
                @pl.when(first < half)
                def _():
                    keep_ref[block_rows, cols] = o

                @pl.when(first >= half)
                def _():
                    send_ref[pl.ds(pl.multiple_of(first - half, BLOCK), BLOCK), cols] = pack(o)

        def arrive(key_pairs, value_pairs):
            def wait():
                for pair in key_pairs:
                    if pair < pairs:
                        copy_of(pair, 0).wait()
                for pair in value_pairs:
                    copy_of(pair, 1).wait()

            wait() if rows == BLOCK else pl.when(block == 0)(wait)

        finish = iter(())
        arrive([0], [])
        for _ in score(0, 0):
            pass
        arrive([1], [0])
        for pair in range(pairs):
            if pair in STAGES:
                until = min([p for p in STAGES if p > pair] + [pairs])
                arrive(range(pair + 1, until + 1), range(pair, until))
            beside = score(pair + 1, (pair + 1) % 2) if pair + 1 < pairs else iter(())
            for head in range(2):
                done = weigh(pair, head, pair % 2, beside, finish)
                finish = place(pair, head, *done)
            for _ in beside:
                pass
        for _ in finish:
            pass

    if rows == BLOCK:
        block_at(0)
    else:
        pl.loop(0, rows // BLOCK)(block_at)
    for block in range(rows // BLOCK):
        logs, powers = jnp.transpose(logs_ref[block]), jnp.transpose(powers_ref[block])
        here = slice(block * BLOCK, min((block + 1) * BLOCK, half))
        kept = max(here.stop - here.start, 0)
        for group in range(GROUPS):
            _, keep_stats_ref, send_ref = results[3 * group : 3 * group + 3]
            if group:
                logs, powers = (pltpu.roll(x, LANES - LANES // GROUPS, 1) for x in (logs, powers))
            if kept:
                keep_stats_ref[here, :] = join_stats(logs[:kept], powers[:kept])
            if kept < BLOCK:
                there = slice(block * BLOCK + kept - half, (block + 1) * BLOCK - half)
                send_ref[there, PART_WIDTH:] = pack_stats(logs[kept:], powers[kept:])


def join_stats(log_sum, power):
    lane = lax.broadcasted_iota(jnp.int32, log_sum.shape, 1)
    return jnp.where(lane < PART, log_sum, pltpu.roll(power, PART, 1))


def halves(rows):
    return [
        jax.ShapeDtypeStruct((rows, PART_WIDTH), jnp.float32),
        jax.ShapeDtypeStruct((rows, LANES), jnp.float32),
        jax.ShapeDtypeStruct((rows, PART_WIDTH + LANES), jnp.int16),
    ]


def attend(order, me, tokens, start, q, k, v, sk, sv):
    vmem = pl.BlockSpec(memory_space=pltpu.VMEM)
    hbm = pl.BlockSpec(memory_space=pltpu.HBM)
    rows, keys, own = q.shape[0], k.shape[0], sk.shape[0]
    pairs = HEADS // 2
    return pl.pallas_call(
        functools.partial(attend_kernel, order),
        in_specs=[pl.BlockSpec(memory_space=pltpu.SMEM), hbm, hbm, vmem, hbm, hbm, vmem, vmem],
        out_specs=[vmem] * (3 * GROUPS),
        out_shape=halves(rows // 2) * GROUPS,
        scratch_shapes=[
            pltpu.VMEM((pairs, keys, PAIR), k.dtype),
            pltpu.VMEM((pairs, keys, PAIR), v.dtype),
            pltpu.SemaphoreType.DMA((pairs, 2)),
            pltpu.VMEM((keys, LANES), jnp.float32),
            pltpu.VMEM((keys + own, PAIR), jnp.float32),
            pltpu.VMEM((keys + own, PAIR), jnp.float32),
            pltpu.VMEM((8, PAIR), jnp.float32),
            pltpu.VMEM((rows // BLOCK, LANES, BLOCK), jnp.float32),
            pltpu.VMEM((rows // BLOCK, LANES, BLOCK), jnp.float32),
            pltpu.SMEM((1,), jnp.int32),
            pltpu.SMEM((1,), jnp.int32),
            pltpu.SemaphoreType.DMA((2,)),
        ],
        compiler_params=pltpu.CompilerParams(vmem_limit_bytes=50 << 20),
        cost_estimate=pl.CostEstimate(
            flops=6 * rows * keys * WIDTH, bytes_accessed=4 * keys * WIDTH, transcendentals=rows * keys * HEADS
        ),
        name="attend",
    )(me.reshape(1), tokens, start, q, k, v, sk, sv)


def merge_kernel(last, before, a_ref, a_stats_ref, b_ref, *outs):
    done, outs = outs[:before], outs[before:]
    for part, ref in enumerate(done):
        outs[0][:, part * PART_WIDTH : (part + 1) * PART_WIDTH] = ref[...]
    a_log = a_stats_ref[...]
    a_power = pltpu.roll(a_log, LANES - PART, 1)
    b_log, b_power = unpack_stats(b_ref[:, PART_WIDTH:])
    rows = a_log.shape[0]
    half = rows if last else rows // 2
    top = jnp.maximum(a_log, b_log)
    a_weight, b_weight = jnp.exp2(a_log - top), jnp.exp2(b_log - top)
    total = a_weight + b_weight
    a_share, b_share = a_weight / total, b_weight / total * (jnp.exp2(b_power) * (1.0 / STEPS))
    if not last:
        power = jnp.maximum(a_power, b_power)
        row = lax.broadcasted_iota(jnp.int32, power.shape, 0)
        steps = jnp.where(row < half, 1.0, jnp.exp2(-power) * STEPS)
        a_share, b_share = a_share * steps, b_share * steps
    for head in range(PART_HEADS):
        cols = slice(head * HEAD_DIM, (head + 1) * HEAD_DIM)
        o = a_ref[:, cols] * a_share[:, head : head + 1] + unpack(b_ref[:, cols]) * b_share[:, head : head + 1]
        place = slice(before * PART_WIDTH + cols.start, before * PART_WIDTH + cols.stop)
        outs[0][:, place] = o[:half].astype(outs[0].dtype)
        if not last:
            outs[2][:, cols] = pack(o[half:])
    if not last:
        log_sum = jnp.maximum(top + jnp.log2(total), LOG_FLOOR)
        outs[1][...] = join_stats(log_sum[:half], power[:half])
        outs[2][:, PART_WIDTH:] = pack_stats(log_sum[half:], power[half:])


def merge(a, a_stats, b, last, done=()):
    rows = a.shape[0]
    shapes = [jax.ShapeDtypeStruct((rows, (len(done) + 1) * PART_WIDTH), jnp.bfloat16)] if last else halves(rows // 2)
    vmem = pl.BlockSpec(memory_space=pltpu.VMEM)
    return pl.pallas_call(
        functools.partial(merge_kernel, last, len(done)),
        in_specs=[vmem] * (3 + len(done)),
        out_specs=[vmem] * len(shapes),
        out_shape=shapes,
        compiler_params=pltpu.CompilerParams(vmem_limit_bytes=16 << 20),
        name="merge",
    )(a, a_stats, b, *done)


def strides(devices):
    order = []
    stride = 2
    while stride < devices:
        order.append(stride)
        stride *= 2
    if len(order) >= 2:
        order = order[1:] + order[:1]
    return order + [1]


def local(devices, queries, cache_keys, cache_values, span_keys, span_values, cache_tokens, span_start):
    order = strides(devices)

    def swap(x, stride):
        return lax.ppermute(x, "seq", [(i, i ^ stride) for i in range(devices)])

    def stack(pieces):
        return lax.optimization_barrier(jnp.concatenate(pieces, axis=0))

    early, late = [], [queries]
    for stride in order:
        got = [swap(piece, stride) for piece in early + late]
        early, late = [stack(early + late) if early else late[0]], [stack(got) if len(got) > 1 else got[0]]
    q = stack(early + late)
    out = attend(
        tuple(order), lax.axis_index("seq"), cache_tokens, span_start, q, cache_keys, cache_values, span_keys, span_values
    )
    held = [out[3 * group : 3 * group + 3] for group in range(GROUPS)]
    for stride in order[:0:-1]:
        held = [merge(keep, stats, swap(send, stride), False) for keep, stats, send in held]
    got = [swap(send, order[0]) for _, _, send in held]
    done = []
    for group in range(GROUPS - 1):
        done.append(merge(held[group][0], held[group][1], got[group], True)[0])
    return merge(held[-1][0], held[-1][1], got[-1], True, done)[0]


def solution(mesh):
    rows = P(("groups", "seq"), None)
    placed = (rows, rows, rows, rows, rows, P("groups"), P("groups"))
    return jax.shard_map(
        functools.partial(local, mesh.shape["seq"]), mesh=mesh, in_specs=placed, out_specs=rows, check_vma=False
    )
```
